256 devices in a mesh: ctx: 128 (over z, y_lo, x, core), head: 2 (over y_hi).
Axes of the slice: x: 4, y: 4 (y_hi: 2, y_lo: 2; y = y_hi * 2 + y_lo), z: 8, core: 2. Of those that a mesh axis runs over, the one named last changes fastest.
Arguments:
- queries: bfloat16 [65536, 4096], P('ctx', 'head'), may hold values from -10 to 10
- key_states: bfloat16 [65536, 1024], P('ctx', 'head'), may hold values from -10 to 10
- value_rows_stored: bfloat16 [65536, 1024], P('ctx', 'head'), may hold values from -6 to 6
- span_order: int32 [128, 4], replicated, may hold values from 0 to 3, each once within a row
- doc_lengths: int32 [128], replicated, may hold values from 1 to 1792, 65536 in all
- w_out: bfloat16 [4096, 4096], P('ctx', 'head'), may hold values from -0.09375 to 0.09375
Outputs:
- projected: bfloat16 [65536, 4096], P('ctx', 'head')
The draws below stay inside these ranges and needn't reach their ends.
Inputs may be any that keep to these rules, and one draw needn't show every extreme that they name: `span_order`: each row is a permutation of 0 to 3, so each shard holds the 4 spans of its own 512 consecutive positions in some order. `doc_lengths`: the lengths sum to 65536; the longest is exactly 1792.
All inputs are finite; a program needn't handle non-finite values.
Results may differ from the reference program's by a relative error of at most 0.0055.
Values may be sent and summed in bfloat16 or wider, within the bound.
A program may use at most 128 MiB of HBM per device.

```python
import math
import jax
import jax.numpy as jnp
import numpy as np
from jax import lax

QUERY_HEADS = 32
KEY_VALUE_HEADS = 8
HEAD_SIZE = 128
D = 4096
SHARD_TOKENS = 512
BLK = 128
PACKED_TOKENS = 65536
CPS = 4
MOST_DOC = 1792
DOCS = 128
REACH = 4
N_CTX = 128


def draw_queries(key, part):
    base_offset = jax.random.fold_in(key, 5)
    gathered_values = jax.random.truncated_normal(base_offset, -6.0, 6.0, (PACKED_TOKENS, QUERY_HEADS * HEAD_SIZE))
    return gathered_values.astype(jnp.bfloat16)


def draw_key_states(key, part):
    base_offset = jax.random.fold_in(key, 9)
    gathered_values = jax.random.truncated_normal(base_offset, -6.0, 6.0, (PACKED_TOKENS, KEY_VALUE_HEADS * HEAD_SIZE))
    return gathered_values.astype(jnp.bfloat16)


def block_scale(rng, extent, cuts, low, high):
    gain, own = 1.0, jax.random.fold_in(rng, 6)
    for axis_at, parts in cuts:
        steps = jnp.exp(jax.random.uniform(jax.random.fold_in(own, axis_at), (parts,), jnp.float32, low / len(cuts), high / len(cuts)))
        gain = gain * jnp.repeat(steps, extent[axis_at] // parts).reshape([-1 if axis == axis_at else 1 for axis in range(len(extent))])
    return gain


def split_up(count, total, reach, skew):
    portions = [(1 << 20) // math.isqrt(standing ** skew) + 1 for standing in range(2, count + 1)]
    surplus, counts = total - reach - (count - 1), [1] * (count - 1)
    while surplus > 0:
        candidates = [i for i in range(count - 1) if counts[i] < reach]
        whole, budget = sum([portions[i] for i in candidates]), surplus
        for i in candidates:
            extra = min(reach - counts[i], max(1, budget * portions[i] // whole), surplus)
            counts[i] = counts[i] + extra
            surplus = surplus - extra
    return np.array([reach] + counts)


def uneven_parts(key, count, total, most, lean):
    if count == 2:
        one = jax.random.randint(key, (), max(1, total - most), min(most, total - 1) + 1)
        return jnp.stack([one, total - one])
    sizes = jnp.asarray(split_up(count, total, most, lean), jnp.int32)
    twos = (count - 1) // 2
    donor, sink = sizes[1:1 + 2 * twos:2], sizes[2:2 + 2 * twos:2]
    room = jnp.minimum(donor - 1, most - sink)
    shifted = jax.random.randint(jax.random.fold_in(key, 1), (twos,), 0, 1 << 20) % (room + 1)
    sizes = sizes.at[1:1 + 2 * twos:2].set(donor - shifted).at[2:2 + 2 * twos:2].set(sink + shifted)
    return sizes[jax.random.permutation(jax.random.fold_in(key, 2), count)]


def bell_draw(own_key, shape, spread, limit, pieces=(), kind=jnp.bfloat16):
    level = block_scale(own_key, shape, pieces, -0.22, 0.18) if pieces else 1.0
    values = jax.random.normal(own_key, shape, jnp.float32) * spread * level
    return jnp.minimum(jnp.maximum(values, -limit), limit).astype(kind)


def setup_inputs(seed: int = 0) -> dict:
    streams_of = jax.random.split(jax.random.key(seed), 7)
    queries = draw_queries(jax.random.fold_in(streams_of[6], 71), 0)
    key_states = draw_key_states(jax.random.fold_in(streams_of[6], 71), 0)
    value_rows_stored = bell_draw(streams_of[2], (PACKED_TOKENS, KEY_VALUE_HEADS * HEAD_SIZE), 1.0, 6.0, ((0, 128), (1, 2)))
    span_order = jax.vmap(lambda own: jax.random.permutation(own, CPS))(jax.random.split(streams_of[3], N_CTX)).reshape((N_CTX, CPS)).astype(jnp.int32)
    doc_lengths = uneven_parts(streams_of[4], DOCS, PACKED_TOKENS, MOST_DOC, 2).astype(jnp.int32)
    w_out = bell_draw(streams_of[5], (QUERY_HEADS * HEAD_SIZE, D), (QUERY_HEADS * HEAD_SIZE) ** -0.5, 0.09375, ((0, 128), (1, 2)))
    return dict(queries=queries, key_states=key_states, value_rows_stored=value_rows_stored, span_order=span_order, doc_lengths=doc_lengths, w_out=w_out)


def stored_positions(span_order):
    stored = jnp.arange(PACKED_TOKENS, dtype=jnp.int32)
    shard_index = stored // SHARD_TOKENS
    slot_index = stored % SHARD_TOKENS // BLK
    return shard_index * SHARD_TOKENS + span_order[shard_index, slot_index].astype(jnp.int32) * BLK + stored % BLK

def reference(queries, key_states, value_rows_stored, span_order, doc_lengths, w_out):
    positions = stored_positions(span_order)
    inverse = jnp.zeros((PACKED_TOKENS,), jnp.int32).at[positions].set(jnp.arange(PACKED_TOKENS, dtype=jnp.int32))
    ordered_q = queries[inverse]
    sorted_keys = key_states[inverse]
    sorted_values = value_rows_stored[inverse]
    ends = jnp.cumsum(doc_lengths).astype(jnp.int32)
    sequence = jnp.arange(PACKED_TOKENS, dtype=jnp.int32)
    doc_ids = jnp.searchsorted(ends, sequence, side='right').astype(jnp.int32)
    visible_window = REACH * SHARD_TOKENS
    queries_per_group = QUERY_HEADS // KEY_VALUE_HEADS
    padded_keys = jnp.concatenate([jnp.zeros((visible_window, KEY_VALUE_HEADS * HEAD_SIZE), jnp.bfloat16), sorted_keys], axis=0)
    padded_values = jnp.concatenate([jnp.zeros((visible_window, KEY_VALUE_HEADS * HEAD_SIZE), jnp.bfloat16), sorted_values], axis=0)
    pad_docs = jnp.concatenate([jnp.full((visible_window,), -1, jnp.int32), doc_ids], axis=0)

    def block(index):
        start = index * SHARD_TOKENS
        query_tile_rows = lax.dynamic_slice_in_dim(ordered_q, start, SHARD_TOKENS, 0).astype(jnp.float32)
        query_tile_rows = query_tile_rows.reshape(SHARD_TOKENS, KEY_VALUE_HEADS, queries_per_group, HEAD_SIZE)
        key_tile_rows = lax.dynamic_slice_in_dim(padded_keys, start, visible_window + SHARD_TOKENS, 0).astype(jnp.float32)
        key_tile_rows = key_tile_rows.reshape(visible_window + SHARD_TOKENS, KEY_VALUE_HEADS, HEAD_SIZE)
        value_tile_rows = lax.dynamic_slice_in_dim(padded_values, start, visible_window + SHARD_TOKENS, 0).astype(jnp.float32)
        value_tile_rows = value_tile_rows.reshape(visible_window + SHARD_TOKENS, KEY_VALUE_HEADS, HEAD_SIZE)
        key_docs = lax.dynamic_slice_in_dim(pad_docs, start, visible_window + SHARD_TOKENS, 0)
        key_pos = start - visible_window + jnp.arange(visible_window + SHARD_TOKENS, dtype=jnp.int32)
        query_pos = start + jnp.arange(SHARD_TOKENS, dtype=jnp.int32)
        query_docs = lax.dynamic_slice_in_dim(doc_ids, start, SHARD_TOKENS, 0)
        visible = (query_docs[:, None] == key_docs[None, :]) & (key_pos[None, :] <= query_pos[:, None])
        scores = jnp.einsum('qhgd,khd->hgqk', query_tile_rows, key_tile_rows) / math.sqrt(HEAD_SIZE)
        masked = jnp.where(visible[None, None], scores, -1e+30)
        peak = lax.optimization_barrier(jnp.max(masked, axis=-1, keepdims=True))
        weights = jnp.where(visible[None, None], jnp.exp(masked - peak), 0.0)
        totals = lax.optimization_barrier(jnp.sum(weights, axis=-1))
        rounded = lax.optimization_barrier(weights.astype(jnp.bfloat16)).astype(jnp.float32)
        accum = jnp.einsum('hgqk,khd->hgqd', rounded, value_tile_rows)
        result = accum / totals[..., None]
        return result.transpose(2, 0, 1, 3).reshape(SHARD_TOKENS, QUERY_HEADS * HEAD_SIZE).astype(jnp.bfloat16)
    attended = lax.map(block, jnp.arange(PACKED_TOKENS // SHARD_TOKENS, dtype=jnp.int32)).reshape(PACKED_TOKENS, QUERY_HEADS * HEAD_SIZE)
    stored_rows = attended[positions]
    product = jnp.dot(stored_rows.astype(jnp.float32), w_out.astype(jnp.float32), preferred_element_type=jnp.float32)
    return product.astype(jnp.bfloat16)
```

```python
import math

import jax
import jax.numpy as jnp
from jax import lax
from jax.experimental import pallas as pl
from jax.experimental.pallas import tpu as pltpu
from jax.sharding import PartitionSpec as P

MESH = pl.DeviceIdType.MESH
BF16 = jnp.bfloat16
F32 = jnp.float32
HD = 128
BLK = 128
ROWS = 512
NX, NY, NZ = 4, 2, 8
NG = 4
WIN = 15 * BLK
NA = 1280
NB = 2048 - NA
SCALE = math.log2(math.e) / math.sqrt(HD)
NEG = -1e30

AX, AY, AZ, AM = 0, 3, 4, 12
BZ, BY, BX, BM = 21, 28, 29, 32
N_W = 36


def kernel(so_ref, lens_ref, q_ref, k_ref, v_ref, w_ref, out_ref,
           kv, wa, wb, att, acca, accb, st_ref, kvs, kvr, ws, wr, ats, atr):
    c = lax.axis_index("ctx")
    h = lax.axis_index("head")
    core = lax.rem(c, 2)
    chip = lax.div(c, 2)
    x = lax.rem(chip, NX)
    yl = lax.rem(lax.div(chip, NX), NY)
    z = lax.div(chip, NX * NY)

    def dev(z_, y_, x_, core_, h_):
        return (((z_ * NY + y_) * NX + x_) * 2 + core_, h_)

    def along(by, core_):
        return (lax.rem(chip + by + 64, 64) * 2 + core_, h)

    def zz(by):
        return lax.rem(z + by + NZ, NZ)

    def xx(by):
        return lax.rem(x + by + NX, NX)

    mate = (chip * 2 + 1 - core, h)
    xp, xm = dev(z, yl, xx(1), core, h), dev(z, yl, xx(-1), core, h)
    zp, zm = dev(zz(1), yl, x, core, h), dev(zz(-1), yl, x, core, h)
    yo = dev(z, 1 - yl, x, core, h)
    ho = (c, 1 - h)

    barrier = pltpu.get_barrier_semaphore()

    def signal(to):
        pl.semaphore_signal(barrier, inc=1, device_id=to, device_id_type=MESH)

    for to in (mate, xp, xm, zp, zm, yo, ho, along(-1, core)):
        signal(to)

    @pl.when(core == 0)
    def _():
        signal(along(-2, 0))
        signal(along(-2, 1))

    order = [so_ref[c, j] for j in range(4)]

    def held(ref, span, cols):
        parts = [ref[j * BLK:(j + 1) * BLK, cols] for j in range(4)]
        part = parts[3]
        for j in (2, 1, 0):
            part = jnp.where(order[j] == span, parts[j], part)
        return part

    for b in range(4):
        for g in range(NG):
            at = pl.ds((14 + b) * BLK, BLK)
            kv[g, at, 0:HD] = held(k_ref, b, slice(g * HD, (g + 1) * HD))
            kv[g, at, HD:2 * HD] = held(v_ref, b, slice(g * HD, (g + 1) * HD))
    wa[z, yl, x, core] = w_ref[:, 0:NA]
    wb[z, yl, x, core] = w_ref[:, NA:2048]

    lens = lens_ref[...]
    high = lax.div(lens, 64)
    low = lens - high * 64
    upto = (lax.broadcasted_iota(jnp.int32, (128, 128), 0)
            <= lax.broadcasted_iota(jnp.int32, (128, 128), 1)).astype(F32).astype(BF16)

    def running(part):
        wide = jnp.broadcast_to(part.astype(F32), (16, 128)).astype(BF16)
        return jnp.dot(wide, upto, preferred_element_type=F32)[0:1, :]

    ends = running(high) * 64.0 + running(low)
    pos = (lax.broadcasted_iota(jnp.int32, (ROWS, 128), 0) + c * ROWS).astype(F32)
    begun = jnp.where(ends <= pos, ends, 0.0)
    first = jnp.max(begun, axis=1, keepdims=True)
    blk = lax.div(lax.broadcasted_iota(jnp.int32, (ROWS, 128), 0), BLK)
    origin = (blk * BLK + (c * ROWS - 14 * BLK)).astype(F32)
    st_ref[...] = jnp.broadcast_to(first, (ROWS, 128)) - origin

    acca[...] = jnp.zeros_like(acca)
    accb[...] = jnp.zeros_like(accb)

    pl.semaphore_wait(barrier, 9)

    def kv_at(g, tile, tiles):
        return kv.at[g, pl.ds(tile * BLK, tiles * BLK)]

    def kv_copy(g, src, dst, tiles, number, slot, to):
        return pltpu.make_async_remote_copy(
            src_ref=kv_at(g, src, tiles), dst_ref=kv_at(g, dst, tiles),
            send_sem=kvs.at[g, number], recv_sem=kvr.at[g, slot],
            device_id=to, device_id_type=MESH)

    def near0(g):
        return [kv_copy(g, 14, 6, 4, 0, 1, along(1, 0)),
                kv_copy(g, 14, 10, 4, 1, 0, mate),
                kv_copy(g, 16, 0, 2, 2, 3, along(2, 0))]

    def near1(g):
        return [kv_copy(g, 14, 6, 4, 0, 1, along(1, 1)),
                kv_copy(g, 14, 2, 4, 2, 2, along(2, 0))]

    def pass0(g):
        return [kv_copy(g, 6, 2, 4, 3, 2, mate), kv_copy(g, 4, 0, 2, 4, 3, mate)]

    def pass1(g):
        return [kv_copy(g, 6, 10, 4, 3, 0, mate)]

    def kv_wait(g, slot):
        tile, tiles = ((10, 4), (6, 4), (2, 4), (0, 2))[slot]
        kv_copy(g, tile, tile, tiles, 0, slot, mate).wait_recv()

    def kv_send(g):
        @pl.when(core == 0)
        def _():
            for copy in near0(g):
                copy.start()

        @pl.when(core == 1)
        def _():
            for copy in near1(g):
                copy.start()

    def kv_pass(g):
        @pl.when(core == 0)
        def _():
            one, two = pass0(g)
            kv_wait(g, 1)
            one.start()
            kv_wait(g, 2)
            two.start()

        @pl.when(core == 1)
        def _():
            kv_wait(g, 1)
            for copy in pass1(g):
                copy.start()

    def kv_rest(g):
        @pl.when(core == 0)
        def _():
            kv_wait(g, 0)
            kv_wait(g, 3)

        @pl.when(core == 1)
        def _():
            kv_wait(g, 0)
            kv_wait(g, 2)
            kv_wait(g, 3)

    def kv_drain(g):
        @pl.when(core == 0)
        def _():
            for copy in near0(g) + pass0(g):
                copy.wait_send()

        @pl.when(core == 1)
        def _():
            for copy in near1(g) + pass1(g):
                copy.wait_send()

    def put(part, number, to, src=None):
        return lambda: pltpu.make_async_remote_copy(
            src_ref=part if src is None else src, dst_ref=part,
            send_sem=ws.at[number], recv_sem=wr.at[number], device_id=to, device_id_type=MESH)

    def entry(part, number, to, got_part, src=None):
        return put(part, number, to, src), number, got_part

    def a_block(x_):
        return wa.at[z, yl, x_, core]

    def a_row(y_):
        return wa.at[z, y_, :, core]

    def a_group(z_, core_=None):
        return wa.at[z_, :, :, core if core_ is None else core_]

    def a_half(z_, y_, core_=None):
        return wa.at[z_, y_, :, core if core_ is None else core_]

    def b_block(z_):
        return wb.at[z_, yl, x, core]

    def b_line(y_):
        return wb.at[:, y_, x, core]

    def b_group(x_, core_=None):
        return wb.at[:, :, x_, core if core_ is None else core_]

    own_a, own_b = w_ref.at[:, pl.ds(0, NA)], w_ref.at[:, pl.ds(NA, NB)]
    ax = [entry(a_block(x), AX, xp, a_block(xx(-1)), own_a),
          entry(a_block(x), AX + 1, xm, a_block(xx(1)), own_a),
          entry(a_block(xx(1)), AX + 2, xm, a_block(xx(2)))]
    ay = entry(a_row(yl), AY, yo, a_row(1 - yl))
    az = []
    for s in range(3):
        az.append(entry(a_group(zz(-s)), AZ + 2 * s, zp, a_group(zz(-s - 1))))
        az.append(entry(a_group(zz(s)), AZ + 2 * s + 1, zm, a_group(zz(s + 1))))
    az.append(entry(a_half(zz(-3), 0), AZ + 6, zp, a_half(zz(-4), 0)))
    az.append(entry(a_half(zz(3), 1), AZ + 7, zm, a_half(zz(4), 1)))
    am = [entry(a_group(z), AM, mate, a_group(z, 1 - core))]
    for s in range(3):
        am.append(entry(a_group(zz(-s - 1)), AM + 1 + 2 * s, mate, a_group(zz(-s - 1), 1 - core)))
        am.append(entry(a_group(zz(s + 1)), AM + 2 + 2 * s, mate, a_group(zz(s + 1), 1 - core)))
    am.append(entry(a_half(zz(4), 0), AM + 7, mate, a_half(zz(4), 0, 1 - core)))
    am.append(entry(a_half(zz(4), 1), AM + 8, mate, a_half(zz(4), 1, 1 - core)))
    bz = []
    for s in range(3):
        up_src = own_b if s == 0 else None
        bz.append(entry(b_block(zz(-s)), BZ + 2 * s, zp, b_block(zz(-s - 1)), up_src))
        bz.append(entry(b_block(zz(s)), BZ + 2 * s + 1, zm, b_block(zz(s + 1)), up_src))
    bz.append(entry(b_block(zz(-3)), BZ + 6, zp, b_block(zz(-4))))
    by = entry(b_line(yl), BY, yo, b_line(1 - yl))
    bx = [entry(b_group(x), BX, xp, b_group(xx(-1))),
          entry(b_group(x), BX + 1, xm, b_group(xx(1))),
          entry(b_group(xx(1)), BX + 2, xm, b_group(xx(2)))]
    bm = [entry(b_group(xx(d)), BM + i, mate, b_group(xx(d), 1 - core))
          for i, d in enumerate((0, -1, 1, 2))]

    def go(*entries):
        for copy, _, _ in entries:
            copy().start()

    def got(*entries):
        for _, number, part in entries:
            put(part, number, mate)().wait_recv()

    def att_copy(head, g, b):
        part = att.at[4 * head + g, pl.ds(b * BLK, BLK)]
        return pltpu.make_async_remote_copy(
            src_ref=part, dst_ref=part, send_sem=ats.at[g, b], recv_sem=atr.at[g, b],
            device_id=ho, device_id_type=MESH)

    go(ax[0], ax[1], bz[0], bz[1])
    kv_send(0)
    got(ax[1])
    go(ax[2])
    got(bz[0], bz[1])
    go(bz[2], bz[3])
    kv_send(1)
    got(ax[0], ax[2])
    go(ay)
    got(bz[2], bz[3])
    go(bz[4], bz[5])
    kv_send(2)
    got(bz[4], bz[5])
    go(bz[6])
    kv_send(3)
    got(bz[6])
    go(by)
    kv_pass(0)

    def ev_az1():
        got(ay)
        go(az[0], az[1], am[0])

    def ev_bx1():
        got(by)
        go(bx[0], bx[1], bm[0])

    def ev_az(s):
        def run():
            got(az[2 * s - 2], az[2 * s - 1])
            go(az[2 * s], az[2 * s + 1], am[2 * s - 1], am[2 * s])
        return run

    def ev_bx2():
        got(bx[1])
        go(bx[2], bm[2])

    def ev_kv(g):
        return lambda: kv_pass(g)

    before = {0: [ev_az1], 3: [ev_kv(1)], 4: [ev_bx1], 6: [ev_az(1)], 7: [ev_kv(2)],
              10: [ev_bx2], 11: [ev_kv(3)], 12: [ev_az(2)]}

    lane = lax.broadcasted_iota(jnp.int32, (BLK, WIN), 1).astype(F32)
    row = lax.broadcasted_iota(jnp.int32, (BLK, BLK), 0)
    causal = lax.broadcasted_iota(jnp.int32, (BLK, BLK), 1) <= row

    def unit(i, carry):
        g, b = lax.div(i, 4), lax.rem(i, 4)
        for at, runs in before.items():
            @pl.when(i == at)
            def _(runs=runs):
                for run in runs:
                    run()

        @pl.when(b == 0)
        def _():
            kv_rest(g)

        @pl.when(i > 0)
        def _():
            att_copy(h, lax.div(i - 1, 4), lax.rem(i - 1, 4)).start()

        q4 = held(q_ref, b, pl.ds(pl.multiple_of(g * 4 * HD, 4 * HD), 4 * HD))
        q = jnp.concatenate([q4[:, j * HD:(j + 1) * HD] for j in range(4)], axis=0)
        window = pl.ds(pl.multiple_of(b * BLK, BLK), WIN)
        k = kv[g, window, 0:HD]
        v = kv[g, window, HD:2 * HD]
        s = lax.dot_general(q, k, (((1,), (1,)), ((), ())), preferred_element_type=F32)
        st = st_ref[pl.ds(pl.multiple_of(b * BLK, BLK), BLK), :]
        far = lane[:, :14 * BLK] >= jnp.concatenate([st] * 14, axis=1)
        last = (lane[:, 14 * BLK:] >= st) & causal
        far4 = jnp.concatenate([far] * 4, axis=0)
        last4 = jnp.concatenate([last] * 4, axis=0)
        s = jnp.concatenate([jnp.where(far4, s[:, :14 * BLK], NEG),
                             jnp.where(last4, s[:, 14 * BLK:], NEG)], axis=1)
        m = jnp.max(s, axis=1, keepdims=True)
        p = jnp.exp2((s - m) * SCALE).astype(BF16)
        vo = jnp.concatenate([v, jnp.ones((WIN, HD), BF16)], axis=1)
        o = jnp.dot(p, vo, preferred_element_type=F32)
        a = (o[:, :HD] / o[:, HD:]).astype(BF16)
        a4 = jnp.concatenate([a[j * BLK:(j + 1) * BLK] for j in range(4)], axis=1)
        att[4 * h + g, pl.ds(pl.multiple_of(b * BLK, BLK), BLK), :] = a4
        return carry

    lax.fori_loop(0, 16, unit, 0)
    att_copy(h, 3, 3).start()

    got(az[4], az[5])
    go(az[6], az[7], am[5], am[6])
    got(bx[0])
    go(bm[1])
    got(bx[2])
    go(bm[3])
    got(az[6], az[7])
    go(am[7], am[8])
    got(*am)
    got(*bm)

    def project(j, carry):
        at = lax.rem(4 * h + j, 8)

        @pl.when(j >= 4)
        def _():
            for b in range(4):
                att_copy(1 - h, j - 4, b).wait_recv()

        a = att[at]
        acca[...] += jnp.dot(a, wa[at].reshape(ROWS, NA), preferred_element_type=F32)
        accb[...] += jnp.dot(a, wb[at].reshape(ROWS, NB), preferred_element_type=F32)
        return carry

    lax.fori_loop(0, 8, project, 0)
    def placed(ref, j):
        part = ref[3 * BLK:4 * BLK, :]
        for b in (2, 1, 0):
            part = jnp.where(order[j] == b, ref[b * BLK:(b + 1) * BLK, :], part)
        return part.astype(BF16)

    for j in range(4):
        out_ref[j * BLK:(j + 1) * BLK, 0:NA] = placed(acca, j)
        out_ref[j * BLK:(j + 1) * BLK, NA:2048] = placed(accb, j)

    for g in range(NG):
        kv_drain(g)
        for b in range(4):
            att_copy(h, g, b).wait_send()
    for copy, _, _ in ax + [ay] + az + am + bz + [by] + bx + bm:
        copy().wait_send()


def per_device(queries, key_states, value_rows_stored, span_order, doc_lengths, w_out):
    vmem = pl.BlockSpec(memory_space=pltpu.VMEM)
    return pl.pallas_call(
        kernel,
        out_shape=jax.ShapeDtypeStruct((ROWS, 2048), BF16),
        in_specs=[pl.BlockSpec(memory_space=pltpu.SMEM), vmem, vmem, vmem, vmem, vmem],
        out_specs=vmem,
        scratch_shapes=[
            pltpu.VMEM((NG, 18 * BLK, 2 * HD), BF16),
            pltpu.VMEM((NZ, NY, NX, 2, 32, NA), BF16),
            pltpu.VMEM((NZ, NY, NX, 2, 32, NB), BF16),
            pltpu.VMEM((8, ROWS, 4 * HD), BF16),
            pltpu.VMEM((ROWS, NA), F32),
            pltpu.VMEM((ROWS, NB), F32),
            pltpu.VMEM((ROWS, 128), F32),
            pltpu.SemaphoreType.DMA((NG, 5)),
            pltpu.SemaphoreType.DMA((NG, 4)),
            pltpu.SemaphoreType.DMA((N_W,)),
            pltpu.SemaphoreType.DMA((N_W,)),
            pltpu.SemaphoreType.DMA((NG, 4)),
            pltpu.SemaphoreType.DMA((NG, 4)),
        ],
        compiler_params=pltpu.CompilerParams(
            collective_id=0, has_side_effects=True, vmem_limit_bytes=63 * 1024 * 1024),
        name="attend_project",
    )(span_order, doc_lengths.reshape(1, 128), queries, key_states, value_rows_stored, w_out)


def solution(mesh):
    placed = (P("ctx", "head"), P("ctx", "head"), P("ctx", "head"), P(), P(), P("ctx", "head"))
    return jax.shard_map(
        per_device, mesh=mesh, in_specs=placed, out_specs=P("ctx", "head"), check_vma=False
    )
```

```python
import math

import jax
import jax.numpy as jnp
from jax import lax
from jax.experimental import pallas as pl
from jax.experimental.pallas import tpu as pltpu
from jax.sharding import PartitionSpec as P

MESH = pl.DeviceIdType.MESH
BF16 = jnp.bfloat16
F32 = jnp.float32
HD = 128
BLK = 128
ROWS = 512
NX, NY, NZ = 4, 2, 8
NG = 4
WIN = 15 * BLK
NA = 1024
NB = 2048 - NA
SCALE = math.log2(math.e) / math.sqrt(HD)
NEG = -1e30

AX, AY, AZ, AM = 0, 3, 4, 32
BZ, BY, BX, BM = 40, 47, 48, 72
N_W = 76
VIA = (2, 3)


def kernel(so_ref, lens_ref, q_hbm, k_ref, v_ref, w_ref, out_ref,
           q_ref, kv, transit, wa, wb, att, acca, accb, st_ref, kvs, kvr, ts, tr, ws, wr, ats, atr, q_sem):
    q_copy = pltpu.make_async_copy(q_hbm, q_ref, q_sem)
    q_copy.start()
    c = lax.axis_index("ctx")
    h = lax.axis_index("head")
    core = lax.rem(c, 2)
    chip = lax.div(c, 2)
    x = lax.rem(chip, NX)
    yl = lax.rem(lax.div(chip, NX), NY)
    z = lax.div(chip, NX * NY)

    def dev(z_, y_, x_, core_, h_):
        return (((z_ * NY + y_) * NX + x_) * 2 + core_, h_)

    def along(by, core_):
        return (lax.rem(chip + by + 64, 64) * 2 + core_, h)

    def zz(by):
        return lax.rem(z + by + NZ, NZ)

    def xx(by):
        return lax.rem(x + by + NX, NX)

    mate = (chip * 2 + 1 - core, h)
    xp, xm = dev(z, yl, xx(1), core, h), dev(z, yl, xx(-1), core, h)
    zp, zm = dev(zz(1), yl, x, core, h), dev(zz(-1), yl, x, core, h)
    yo = dev(z, 1 - yl, x, core, h)
    ho = (c, 1 - h)

    barrier = pltpu.get_barrier_semaphore()

    def signal(to):
        pl.semaphore_signal(barrier, inc=1, device_id=to, device_id_type=MESH)

    for to in (mate, xp, xm, zp, zm, yo, ho, along(-1, core)):
        signal(to)

    @pl.when(core == 0)
    def _():
        signal(along(-1, 1))

    @pl.when(x == 0)
    def _():
        signal(along(-4, core))

    order = [so_ref[j, c] for j in range(4)]

    def held(ref, span, cols):
        parts = [ref[j * BLK:(j + 1) * BLK, cols] for j in range(4)]
        part = parts[3]
        for j in (2, 1, 0):
            part = jnp.where(order[j] == span, parts[j], part)
        return part

    for b in range(4):
        for g in range(NG):
            at = pl.ds((14 + b) * BLK, BLK)
            kv[g, at, 0:HD] = held(k_ref, b, slice(g * HD, (g + 1) * HD))
            kv[g, at, HD:2 * HD] = held(v_ref, b, slice(g * HD, (g + 1) * HD))
    wa[z, yl, x, core] = w_ref[:, 0:NA]
    wb[z, yl, x, core] = w_ref[:, NA:2048]

    lens = lens_ref[...]
    high = lax.div(lens, 64)
    low = lens - high * 64
    upto = (lax.broadcasted_iota(jnp.int32, (128, 128), 0)
            <= lax.broadcasted_iota(jnp.int32, (128, 128), 1)).astype(F32).astype(BF16)

    def running(part):
        wide = jnp.broadcast_to(part.astype(F32), (16, 128)).astype(BF16)
        return jnp.dot(wide, upto, preferred_element_type=F32)[0:1, :]

    ends = running(high) * 64.0 + running(low)
    pos = (lax.broadcasted_iota(jnp.int32, (ROWS, 128), 0) + c * ROWS).astype(F32)
    begun = jnp.where(ends <= pos, ends, 0.0)
    first = jnp.max(begun, axis=1, keepdims=True)
    blk = lax.div(lax.broadcasted_iota(jnp.int32, (ROWS, 128), 0), BLK)
    origin = (blk * BLK + (c * ROWS - 14 * BLK)).astype(F32)
    st_ref[...] = jnp.broadcast_to(first, (ROWS, 128)) - origin

    acca[...] = jnp.zeros_like(acca)
    accb[...] = jnp.zeros_like(accb)

    pl.semaphore_wait(barrier, 8 + core + jnp.where(x == 0, 1, 0))

    def kv_at(g, tile, tiles):
        return kv.at[g, pl.ds(tile * BLK, tiles * BLK)]

    def kv_copy(g, src, dst, tiles, number, slot, to):
        return pltpu.make_async_remote_copy(
            src_ref=kv_at(g, src, tiles), dst_ref=kv_at(g, dst, tiles),
            send_sem=kvs.at[g, number], recv_sem=kvr.at[g, slot],
            device_id=to, device_id_type=MESH)

    def own_near(g):
        return kv_copy(g, 14, 6, 4, 0, 1, along(1, core))

    def own_via(g):
        return pltpu.make_async_remote_copy(
            src_ref=kv_at(g, 14, 4), dst_ref=transit.at[VIA.index(g)],
            send_sem=kvs.at[g, 0], recv_sem=tr.at[VIA.index(g)], device_id=xp, device_id_type=MESH)

    def own_on(g):
        return pltpu.make_async_remote_copy(
            src_ref=transit.at[VIA.index(g)], dst_ref=kv_at(g, 6, 4),
            send_sem=ts.at[VIA.index(g)], recv_sem=kvr.at[g, 1], device_id=along(4, core),
            device_id_type=MESH)

    def own_mate(g):
        return kv_copy(g, 14, 10, 4, 1, 0, mate)

    def pass0(g):
        return [kv_copy(g, 8, 0, 2, 2, 3, along(1, 0)), kv_copy(g, 6, 2, 4, 3, 2, mate)]

    def pass1(g):
        return [kv_copy(g, 6, 2, 4, 2, 2, along(1, 0)), kv_copy(g, 6, 10, 4, 3, 0, mate)]

    def late0(g):
        return kv_copy(g, 4, 0, 2, 4, 3, mate)

    def kv_wait(g, slot):
        tile, tiles = ((10, 4), (6, 4), (2, 4), (0, 2))[slot]
        kv_copy(g, tile, tile, tiles, 0, slot, mate).wait_recv()

    def kv_send(g):
        if g in VIA:
            @pl.when(x < 3)
            def _():
                own_near(g).start()
        else:
            own_near(g).start()

        @pl.when(core == 0)
        def _():
            own_mate(g).start()

    def kv_via(g):
        @pl.when(x == 3)
        def _():
            own_via(g).start()

    def kv_on(g):
        @pl.when(x == 0)
        def _():
            own_via(g).wait_recv()
            own_on(g).start()

    def kv_pass(g):
        kv_wait(g, 1)

        @pl.when(core == 0)
        def _():
            for copy in pass0(g):
                copy.start()

        @pl.when(core == 1)
        def _():
            for copy in pass1(g):
                copy.start()

    def kv_late(g):
        kv_wait(g, 2)

        @pl.when(core == 0)
        def _():
            late0(g).start()

    def kv_rest(g):
        kv_wait(g, 0)
        kv_wait(g, 3)

    def kv_drain(g):
        own_near(g).wait_send()
        if g in VIA:
            @pl.when(x == 0)
            def _():
                own_on(g).wait_send()

        @pl.when(core == 0)
        def _():
            for copy in [own_mate(g)] + pass0(g) + [late0(g)]:
                copy.wait_send()

        @pl.when(core == 1)
        def _():
            for copy in pass1(g):
                copy.wait_send()

    def put(part, number, to, src=None):
        return lambda: pltpu.make_async_remote_copy(
            src_ref=part if src is None else src, dst_ref=part,
            send_sem=ws.at[number], recv_sem=wr.at[number], device_id=to, device_id_type=MESH)

    def entry(part, number, to, got_part, src=None):
        return put(part, number, to, src), number, got_part

    def a_block(y_):
        return wa.at[z, y_, x, core]

    def a_pair(x_):
        return wa.at[z, :, x_, core]

    def a_group(z_, core_=None):
        return wa.at[z_, :, :, core if core_ is None else core_]

    def b_block(y_):
        return wb.at[z, y_, x, core]

    def b_pair(z_):
        return wb.at[z_, :, x, core]

    def b_group(x_, core_=None):
        return wb.at[:, :, x_, core if core_ is None else core_]

    own_a, own_b = w_ref.at[:, pl.ds(0, NA)], w_ref.at[:, pl.ds(NA, NB)]
    ay = entry(a_block(yl), AY, yo, a_block(1 - yl), own_a)
    by = entry(b_block(yl), BY, yo, b_block(1 - yl), own_b)
    ax = [entry(a_pair(x), AX, xp, a_pair(xx(-1))),
          entry(a_pair(x), AX + 1, xm, a_pair(xx(1))),
          entry(a_pair(xx(1)), AX + 2, xm, a_pair(xx(2)))]
    xq = (x, xx(-1), xx(1), xx(2))

    def az(qs, s):
        def part(d, q):
            return wa.at[zz(d), :, xq[q], core]
        if s == 3:
            return [entry(part(3, q), AZ + 7 * q + 6, zm, part(4, q)) for q in qs]
        return ([entry(part(-s, q), AZ + 7 * q + 2 * s, zp, part(-s - 1, q)) for q in qs]
                + [entry(part(s, q), AZ + 7 * q + 2 * s + 1, zm, part(s + 1, q)) for q in qs])

    def bz(s):
        if s == 3:
            return [entry(b_pair(zz(3)), BZ + 6, zm, b_pair(zz(4)))]
        return [entry(b_pair(zz(-s)), BZ + 2 * s, zp, b_pair(zz(-s - 1))),
                entry(b_pair(zz(s)), BZ + 2 * s + 1, zm, b_pair(zz(s + 1)))]

    near = (0, -1, 1, -2, 2, -3, 3, 4)
    am = [entry(a_group(zz(d)), AM + i, mate, a_group(zz(d), 1 - core)) for i, d in enumerate(near)]

    def bx(js, way):
        def part(j, d):
            return wb.at[zz(near[j]), :, xx(d), core]
        if way == 0:
            return [entry(part(j, 0), BX + 3 * j, xp, part(j, -1)) for j in js]
        if way == 1:
            return [entry(part(j, 0), BX + 3 * j + 1, xm, part(j, 1)) for j in js]
        return [entry(part(j, 1), BX + 3 * j + 2, xm, part(j, 2)) for j in js]

    bm = [entry(b_group(xx(d)), BM + i, mate, b_group(xx(d), 1 - core))
          for i, d in enumerate((0, -1, 1, 2))]

    def go(*entries):
        for copy, _, _ in entries:
            copy().start()

    def got(*entries):
        for _, number, part in entries:
            put(part, number, mate)().wait_recv()

    def att_copy(head, g, b):
        part = att.at[4 * head + g, pl.ds(b * BLK, BLK)]
        return pltpu.make_async_remote_copy(
            src_ref=part, dst_ref=part, send_sem=ats.at[g, b], recv_sem=atr.at[g, b],
            device_id=ho, device_id_type=MESH)

    go(ay, by)
    kv_send(0)
    kv_send(1)
    got(ay, by)
    go(ax[1], *bz(0), *az((0,), 0), *bx((0,), 1))
    kv_pass(0)
    go(ax[0])
    kv_send(2)
    kv_via(2)
    got(ax[1])
    go(ax[2], *az((2,), 0))
    got(*bz(0))
    go(*bz(1), *bx((1, 2), 1))
    kv_pass(1)
    kv_send(3)
    kv_via(3)
    got(*bz(1))
    go(*bz(2), *bx((3, 4), 1))
    got(ax[2])
    go(*az((3,), 0))
    q_copy.wait()
    kv_late(0)

    def at1():
        got(*bz(2))
        go(*bz(3), *bx((5, 6), 1))
        got(*az((0,), 0))
        go(*az((0,), 1))
        got(ax[0])
        go(*az((1,), 0), am[0])

    def at2():
        kv_on(2)
        got(*bz(3))
        go(*bx((7,), 1), bm[0])

    def at3():
        kv_late(1)
        got(*az((2, 3), 0))
        go(*az((2, 3), 1))

    def at4():
        kv_pass(2)
        got(*az((1,), 0))
        go(*az((1,), 1), am[1], am[2])

    def at5():
        kv_on(3)
        got(*bx((0, 1, 2, 3), 1))
        go(*bx((0, 1, 2, 3), 2))

    def at6():
        got(*az((0, 2), 1))
        go(*az((0, 2), 2))

    def at7():
        kv_late(2)
        got(*az((3, 1), 1))
        go(*az((3, 1), 2), am[3], am[4])

    def at8():
        kv_pass(3)
        got(*bx((4, 5, 6, 7), 1))
        go(*bx((4, 5, 6, 7), 2), bm[2])
        go(*bx((0, 1, 2, 3), 0))

    def at9():
        got(*az((0, 2), 2))
        go(*az((0, 2), 3))
        go(*bx((4, 5, 6, 7), 0))

    def at11():
        kv_late(3)
        got(*az((3, 1), 2))
        go(*az((3, 1), 3), am[5], am[6])

    before = {1: at1, 2: at2, 3: at3, 4: at4, 5: at5, 6: at6, 7: at7, 8: at8, 9: at9, 11: at11}

    lane = lax.broadcasted_iota(jnp.int32, (BLK, WIN), 1).astype(F32)
    row = lax.broadcasted_iota(jnp.int32, (BLK, BLK), 0)
    causal = lax.broadcasted_iota(jnp.int32, (BLK, BLK), 1) <= row

    def unit(i, carry):
        g, b = lax.div(i, 4), lax.rem(i, 4)
        for at, run in before.items():
            pl.when(i == at)(run)

        @pl.when(b == 0)
        def _():
            kv_rest(g)

        @pl.when(i > 0)
        def _():
            att_copy(h, lax.div(i - 1, 4), lax.rem(i - 1, 4)).start()

        q4 = held(q_ref, b, pl.ds(pl.multiple_of(g * 4 * HD, 4 * HD), 4 * HD))
        q = jnp.concatenate([q4[:, j * HD:(j + 1) * HD] for j in range(4)], axis=0)
        window = pl.ds(pl.multiple_of(b * BLK, BLK), WIN)
        k = kv[g, window, 0:HD]
        v = kv[g, window, HD:2 * HD]
        s = lax.dot_general(q, k, (((1,), (1,)), ((), ())), preferred_element_type=F32)
        st = st_ref[pl.ds(pl.multiple_of(b * BLK, BLK), BLK), :]
        far = lane[:, :14 * BLK] >= jnp.concatenate([st] * 14, axis=1)
        last = (lane[:, 14 * BLK:] >= st) & causal
        far4 = jnp.concatenate([far] * 4, axis=0)
        last4 = jnp.concatenate([last] * 4, axis=0)
        s = jnp.concatenate([jnp.where(far4, s[:, :14 * BLK], NEG),
                             jnp.where(last4, s[:, 14 * BLK:], NEG)], axis=1)
        m = jnp.max(s, axis=1, keepdims=True)
        p = jnp.exp2((s - m) * SCALE).astype(BF16)
        vo = jnp.concatenate([v, jnp.ones((WIN, HD), BF16)], axis=1)
        o = jnp.dot(p, vo, preferred_element_type=F32)
        a = (o[:, :HD] / o[:, HD:]).astype(BF16)
        a4 = jnp.concatenate([a[j * BLK:(j + 1) * BLK] for j in range(4)], axis=1)
        att[4 * h + g, pl.ds(pl.multiple_of(b * BLK, BLK), BLK), :] = a4
        return carry

    lax.fori_loop(0, 16, unit, 0)
    att_copy(h, 3, 3).start()

    def project_a(j, carry):
        d = lax.rem(lax.div(j + 1, 2) * (2 * lax.rem(j, 2) - 1) + 8, 8)
        at = lax.rem(z + 8 - d, 8)

        @pl.when(j == 7)
        def _():
            got(*az((0, 1, 2, 3), 3))
            go(am[7])

        for i in range(8):
            @pl.when(j == i)
            def _(i=i):
                got(am[i])

        @pl.when(lax.div(at, 4) == 1 - h)
        def _():
            for b in range(4):
                att_copy(1 - h, lax.rem(at, 4), b).wait_recv()

        acca[...] += jnp.dot(att[at], wa[at].reshape(ROWS, NA), preferred_element_type=F32)
        return carry

    lax.fori_loop(0, 8, project_a, 0)
    got(*bx(range(8), 2))
    go(bm[3])
    got(*bx(range(8), 0))
    go(bm[1])
    got(*bm)

    def project_b(at, carry):
        accb[...] += jnp.dot(att[at], wb[at].reshape(ROWS, NB), preferred_element_type=F32)
        return carry

    lax.fori_loop(0, 8, project_b, 0)

    def placed(ref, j):
        part = ref[3 * BLK:4 * BLK, :]
        for b in (2, 1, 0):
            part = jnp.where(order[j] == b, ref[b * BLK:(b + 1) * BLK, :], part)
        return part.astype(BF16)

    for j in range(4):
        out_ref[j * BLK:(j + 1) * BLK, 0:NA] = placed(acca, j)
        out_ref[j * BLK:(j + 1) * BLK, NA:2048] = placed(accb, j)

    for g in range(NG):
        kv_drain(g)
        for b in range(4):
            att_copy(h, g, b).wait_send()
    for copy, _, _ in ax + [ay, by] + am + bm:
        copy().wait_send()
    for s in range(4):
        for copy, _, _ in az((0, 1, 2, 3), s) + bz(s):
            copy().wait_send()
    for way in range(3):
        for copy, _, _ in bx(range(8), way):
            copy().wait_send()


def per_device(queries, key_states, value_rows_stored, span_order, doc_lengths, w_out):
    vmem = pl.BlockSpec(memory_space=pltpu.VMEM)
    return pl.pallas_call(
        kernel,
        out_shape=jax.ShapeDtypeStruct((ROWS, 2048), BF16),
        in_specs=[pl.BlockSpec(memory_space=pltpu.SMEM), vmem, pl.BlockSpec(memory_space=pl.ANY), vmem, vmem, vmem],
        out_specs=vmem,
        scratch_shapes=[
            pltpu.VMEM((ROWS, 2048), BF16),
            pltpu.VMEM((NG, 18 * BLK, 2 * HD), BF16),
            pltpu.VMEM((len(VIA), 4 * BLK, 2 * HD), BF16),
            pltpu.VMEM((NZ, NY, NX, 2, 32, NA), BF16),
            pltpu.VMEM((NZ, NY, NX, 2, 32, NB), BF16),
            pltpu.VMEM((8, ROWS, 4 * HD), BF16),
            pltpu.VMEM((ROWS, NA), F32),
            pltpu.VMEM((ROWS, NB), F32),
            pltpu.VMEM((ROWS, 128), F32),
            pltpu.SemaphoreType.DMA((NG, 5)),
            pltpu.SemaphoreType.DMA((NG, 4)),
            pltpu.SemaphoreType.DMA((len(VIA),)),
            pltpu.SemaphoreType.DMA((len(VIA),)),
            pltpu.SemaphoreType.DMA((N_W,)),
            pltpu.SemaphoreType.DMA((N_W,)),
            pltpu.SemaphoreType.DMA((NG, 4)),
            pltpu.SemaphoreType.DMA((NG, 4)),
            pltpu.SemaphoreType.DMA,
        ],
        compiler_params=pltpu.CompilerParams(
            collective_id=0, has_side_effects=True, vmem_limit_bytes=63 * 1024 * 1024),
        name="attend_project",
    )(span_order.T, doc_lengths.reshape(1, 128), queries, key_states, value_rows_stored, w_out)


def solution(mesh):
    placed = (P("ctx", "head"), P("ctx", "head"), P("ctx", "head"), P(), P(), P("ctx", "head"))
    return jax.shard_map(
        per_device, mesh=mesh, in_specs=placed, out_specs=P("ctx", "head"), check_vma=False
    )
```

```python
import math

import jax
import jax.numpy as jnp
from jax import lax
from jax.experimental import pallas as pl
from jax.experimental.pallas import tpu as pltpu
from jax.sharding import PartitionSpec as P

MESH = pl.DeviceIdType.MESH
BF16 = jnp.bfloat16
F32 = jnp.float32
HD = 128
BLK = 128
ROWS = 512
NX, NY, NZ = 4, 2, 8
NG = 4
WIN = 15 * BLK
NA = 1024
NB = 2048 - NA
SCALE = math.log2(math.e) / math.sqrt(HD)
NEG = -1e30

AX, AY, AZ, AM = 0, 3, 4, 32
BZ, BY, BX, BM = 40, 47, 48, 72
N_W = 76
VIA = (3,)
EARLY = 1


def kernel(so_ref, lens_ref, q_hbm, k_ref, v_ref, w_ref, out_ref,
           q_ref, kv, transit, wa, wb, att, acca, accb, st_ref, kvs, kvr, ts, tr, ws, wr, ats, atr, q_sem):
    q_copy = pltpu.make_async_copy(q_hbm, q_ref, q_sem)
    q_copy.start()
    c = lax.axis_index("ctx")
    h = lax.axis_index("head")
    core = lax.rem(c, 2)
    chip = lax.div(c, 2)
    x = lax.rem(chip, NX)
    yl = lax.rem(lax.div(chip, NX), NY)
    z = lax.div(chip, NX * NY)

    def dev(z_, y_, x_, core_, h_):
        return (((z_ * NY + y_) * NX + x_) * 2 + core_, h_)

    def along(by, core_):
        return (lax.rem(chip + by + 64, 64) * 2 + core_, h)

    def zz(by):
        return lax.rem(z + by + NZ, NZ)

    def xx(by):
        return lax.rem(x + by + NX, NX)

    mate = (chip * 2 + 1 - core, h)
    xp, xm = dev(z, yl, xx(1), core, h), dev(z, yl, xx(-1), core, h)
    zp, zm = dev(zz(1), yl, x, core, h), dev(zz(-1), yl, x, core, h)
    yo = dev(z, 1 - yl, x, core, h)
    ho = (c, 1 - h)

    barrier = pltpu.get_barrier_semaphore()

    def signal(to):
        pl.semaphore_signal(barrier, inc=1, device_id=to, device_id_type=MESH)

    for to in (mate, xp, xm, zp, zm, yo, ho, along(-1, core)):
        signal(to)

    @pl.when(core == 0)
    def _():
        signal(along(-1, 1))

    @pl.when(x == 0)
    def _():
        signal(along(-4, core))

    order = [so_ref[j, c] for j in range(4)]

    def held(ref, span, cols):
        parts = [ref[j * BLK:(j + 1) * BLK, cols] for j in range(4)]
        part = parts[3]
        for j in (2, 1, 0):
            part = jnp.where(order[j] == span, parts[j], part)
        return part

    for b in range(4):
        for g in range(NG):
            at = pl.ds((14 + b) * BLK, BLK)
            kv[g, at, 0:HD] = held(k_ref, b, slice(g * HD, (g + 1) * HD))
            kv[g, at, HD:2 * HD] = held(v_ref, b, slice(g * HD, (g + 1) * HD))
    wa[z, yl, x, core] = w_ref[:, 0:NA]
    wb[z, yl, x, core] = w_ref[:, NA:2048]

    lens = lens_ref[...]
    high = lax.div(lens, 64)
    low = lens - high * 64
    upto = (lax.broadcasted_iota(jnp.int32, (128, 128), 0)
            <= lax.broadcasted_iota(jnp.int32, (128, 128), 1)).astype(F32).astype(BF16)

    def running(part):
        wide = jnp.broadcast_to(part.astype(F32), (16, 128)).astype(BF16)
        return jnp.dot(wide, upto, preferred_element_type=F32)[0:1, :]

    ends = running(high) * 64.0 + running(low)
    pos = (lax.broadcasted_iota(jnp.int32, (ROWS, 128), 0) + c * ROWS).astype(F32)
    begun = jnp.where(ends <= pos, ends, 0.0)
    first = jnp.max(begun, axis=1, keepdims=True)
    blk = lax.div(lax.broadcasted_iota(jnp.int32, (ROWS, 128), 0), BLK)
    origin = (blk * BLK + (c * ROWS - 14 * BLK)).astype(F32)
    st_ref[...] = jnp.broadcast_to(first, (ROWS, 128)) - origin

    acca[...] = jnp.zeros_like(acca)
    accb[...] = jnp.zeros_like(accb)

    pl.semaphore_wait(barrier, 8 + core + jnp.where(x == 0, 1, 0))

    def kv_at(g, tile, tiles):
        return kv.at[g, pl.ds(tile * BLK, tiles * BLK)]

    def kv_copy(g, src, dst, tiles, number, slot, to):
        return pltpu.make_async_remote_copy(
            src_ref=kv_at(g, src, tiles), dst_ref=kv_at(g, dst, tiles),
            send_sem=kvs.at[g, number], recv_sem=kvr.at[g, slot],
            device_id=to, device_id_type=MESH)

    def own_near(g):
        return kv_copy(g, 14, 6, 4, 0, 1, along(1, core))

    def own_via(g):
        return pltpu.make_async_remote_copy(
            src_ref=kv_at(g, 14, 4), dst_ref=transit.at[VIA.index(g)],
            send_sem=kvs.at[g, 0], recv_sem=tr.at[VIA.index(g)], device_id=xp, device_id_type=MESH)

    def own_on(g):
        return pltpu.make_async_remote_copy(
            src_ref=transit.at[VIA.index(g)], dst_ref=kv_at(g, 6, 4),
            send_sem=ts.at[VIA.index(g)], recv_sem=kvr.at[g, 1], device_id=along(4, core),
            device_id_type=MESH)

    def own_mate(g):
        return kv_copy(g, 14, 10, 4, 1, 0, mate)

    def pass0(g):
        return [kv_copy(g, 8, 0, 2, 2, 3, along(1, 0)), kv_copy(g, 6, 2, 4, 3, 2, mate)]

    def pass1(g):
        return [kv_copy(g, 6, 2, 4, 2, 2, along(1, 0)), kv_copy(g, 6, 10, 4, 3, 0, mate)]

    def late0(g):
        return kv_copy(g, 4, 0, 2, 4, 3, mate)

    def kv_wait(g, slot):
        tile, tiles = ((10, 4), (6, 4), (2, 4), (0, 2))[slot]
        kv_copy(g, tile, tile, tiles, 0, slot, mate).wait_recv()

    def kv_send(g):
        if g in VIA:
            @pl.when(x < 3)
            def _():
                own_near(g).start()
        else:
            own_near(g).start()

        @pl.when(core == 0)
        def _():
            own_mate(g).start()

    def kv_via(g):
        if g not in VIA:
            return

        @pl.when(x == 3)
        def _():
            own_via(g).start()

    def kv_on(g):
        if g not in VIA:
            return

        @pl.when(x == 0)
        def _():
            own_via(g).wait_recv()
            own_on(g).start()

    def kv_pass(g):
        kv_wait(g, 1)

        @pl.when(core == 0)
        def _():
            for copy in pass0(g):
                copy.start()

        @pl.when(core == 1)
        def _():
            for copy in pass1(g):
                copy.start()

    def kv_late(g):
        kv_wait(g, 2)

        @pl.when(core == 0)
        def _():
            late0(g).start()

    def kv_rest(g):
        kv_wait(g, 0)
        kv_wait(g, 3)

    def kv_drain(g):
        own_near(g).wait_send()
        if g in VIA:
            @pl.when(x == 0)
            def _():
                own_on(g).wait_send()

        @pl.when(core == 0)
        def _():
            for copy in [own_mate(g)] + pass0(g) + [late0(g)]:
                copy.wait_send()

        @pl.when(core == 1)
        def _():
            for copy in pass1(g):
                copy.wait_send()

    def put(part, number, to, src=None):
        return lambda: pltpu.make_async_remote_copy(
            src_ref=part if src is None else src, dst_ref=part,
            send_sem=ws.at[number], recv_sem=wr.at[number], device_id=to, device_id_type=MESH)

    def entry(part, number, to, got_part, src=None):
        return put(part, number, to, src), number, got_part

    def a_block(y_):
        return wa.at[z, y_, x, core]

    def a_pair(x_):
        return wa.at[z, :, x_, core]

    def a_group(z_, core_=None):
        return wa.at[z_, :, :, core if core_ is None else core_]

    def b_block(y_):
        return wb.at[z, y_, x, core]

    def b_pair(z_):
        return wb.at[z_, :, x, core]

    def b_group(x_, core_=None):
        return wb.at[:, :, x_, core if core_ is None else core_]

    own_a, own_b = w_ref.at[:, pl.ds(0, NA)], w_ref.at[:, pl.ds(NA, NB)]
    ay = entry(a_block(yl), AY, yo, a_block(1 - yl), own_a)
    by = entry(b_block(yl), BY, yo, b_block(1 - yl), own_b)
    ax = [entry(a_pair(x), AX, xp, a_pair(xx(-1))),
          entry(a_pair(x), AX + 1, xm, a_pair(xx(1))),
          entry(a_pair(xx(1)), AX + 2, xm, a_pair(xx(2)))]
    xq = (x, xx(-1), xx(1), xx(2))

    def az(qs, s):
        def part(d, q):
            return wa.at[zz(d), :, xq[q], core]
        if s == 3:
            return [entry(part(3, q), AZ + 7 * q + 6, zm, part(4, q)) for q in qs]
        return ([entry(part(-s, q), AZ + 7 * q + 2 * s, zp, part(-s - 1, q)) for q in qs]
                + [entry(part(s, q), AZ + 7 * q + 2 * s + 1, zm, part(s + 1, q)) for q in qs])

    def bz(s):
        if s == 3:
            return [entry(b_pair(zz(3)), BZ + 6, zm, b_pair(zz(4)))]
        return [entry(b_pair(zz(-s)), BZ + 2 * s, zp, b_pair(zz(-s - 1))),
                entry(b_pair(zz(s)), BZ + 2 * s + 1, zm, b_pair(zz(s + 1)))]

    near = (0, -1, 1, -2, 2, -3, 3, 4)
    am = [entry(a_group(zz(d)), AM + i, mate, a_group(zz(d), 1 - core)) for i, d in enumerate(near)]

    def bx(js, way):
        def part(j, d):
            return wb.at[zz(near[j]), :, xx(d), core]
        if way == 0:
            return [entry(part(j, 0), BX + 3 * j, xp, part(j, -1)) for j in js]
        if way == 1:
            return [entry(part(j, 0), BX + 3 * j + 1, xm, part(j, 1)) for j in js]
        return [entry(part(j, 1), BX + 3 * j + 2, xm, part(j, 2)) for j in js]

    bm = [entry(b_group(xx(d)), BM + i, mate, b_group(xx(d), 1 - core))
          for i, d in enumerate((0, -1, 1, 2))]

    def go(*entries):
        for copy, _, _ in entries:
            copy().start()

    def got(*entries):
        for _, number, part in entries:
            put(part, number, mate)().wait_recv()

    def att_copy(head, g, b):
        part = att.at[4 * head + g, pl.ds(b * BLK, BLK)]
        return pltpu.make_async_remote_copy(
            src_ref=part, dst_ref=part, send_sem=ats.at[g, b], recv_sem=atr.at[g, b],
            device_id=ho, device_id_type=MESH)

    go(ay, by)
    kv_send(0)
    kv_send(1)
    got(ay, by)
    go(ax[1], *bz(0), *az((0,), 0), *bx((0,), 1))
    kv_pass(0)
    go(ax[0])
    kv_send(2)
    kv_via(2)
    got(ax[1])
    go(ax[2], *az((2,), 0))
    got(*bz(0))
    go(*bz(1), *bx((1, 2), 1))
    kv_pass(1)
    kv_send(3)
    kv_via(3)
    got(*bz(1))
    go(*bz(2), *bx((3, 4), 1))
    got(ax[2])
    go(*az((3,), 0))
    q_copy.wait()
    kv_late(0)

    def at1():
        got(*bz(2))
        go(*bz(3), *bx((5, 6), 1))
        got(*az((0,), 0))
        go(*az((0,), 1))
        got(ax[0])
        go(*az((1,), 0), am[0])

    def at2():
        got(*bz(3))
        go(*bx((7,), 1), bm[0])
        kv_on(2)

    def at3():
        got(*az((2, 3), 0))
        go(*az((2, 3), 1))
        kv_late(1)

    def at4():
        got(*az((1,), 0))
        go(*az((1,), 1), am[1], am[2])
        got(*bx((0, 1, 2, 3), 1))
        go(*bx((0, 1, 2, 3), 2))
        kv_pass(2)
        go(*bx((0, 1), 0))

    def at5():
        kv_on(3)

    def at6():
        got(*az((0, 2), 1))
        go(*az((0, 2), 2))

    def at7():
        got(*az((3, 1), 1))
        go(*az((3, 1), 2), am[3], am[4])
        got(*bx((4, 5, 6, 7), 1))
        go(*bx((4, 5, 6, 7), 2), bm[2])
        kv_late(2)

    def at8():
        kv_pass(3)
        go(*bx((2, 3, 4, 5, 6, 7), 0))

    def at9():
        got(*az((0, 2), 2))
        go(*az((0, 2), 3))

    def at11():
        got(*az((3, 1), 2))
        go(*az((3, 1), 3), am[5], am[6])
        kv_late(3)

    before = {1: at1, 2: at2, 3: at3, 4: at4, 5: at5, 6: at6, 7: at7, 8: at8, 9: at9, 11: at11}

    def both_parts(g):
        def part(at):
            a = att[at]
            acca[...] += jnp.dot(a, wa[at].reshape(ROWS, NA), preferred_element_type=F32)
            accb[...] += jnp.dot(a, wb[at].reshape(ROWS, NB), preferred_element_type=F32)

        def side(k, carry):
            head = lax.rem(h + k, 2)

            @pl.when(k == 1)
            def _():
                for b in range(4):
                    att_copy(1 - h, g, b).wait_recv()

            part(4 * head + g)
            return carry

        lax.fori_loop(0, 2, side, 0)

    def project_early():
        got(*az((0, 1, 2, 3), 3))
        go(am[7])
        got(*bx(range(8), 2))
        go(bm[3])
        got(*bx(range(8), 0))
        go(bm[1])
        got(*am)
        got(*bm)

        def each(g, carry):
            both_parts(g)
            return carry

        lax.fori_loop(0, 3, each, 0)

    lane = lax.broadcasted_iota(jnp.int32, (BLK, WIN), 1).astype(F32)
    row = lax.broadcasted_iota(jnp.int32, (BLK, BLK), 0)
    causal = lax.broadcasted_iota(jnp.int32, (BLK, BLK), 1) <= row

    def unit(i, carry):
        g, b = lax.div(i, 4), lax.rem(i, 4)
        @pl.when(i > 0)
        def _():
            att_copy(h, lax.div(i - 1, 4), lax.rem(i - 1, 4)).start()

        for at, run in before.items():
            pl.when(i == at)(run)

        @pl.when((i == 12) & (x < EARLY))
        def _():
            project_early()


        @pl.when(b == 0)
        def _():
            kv_rest(g)

        q4 = held(q_ref, b, pl.ds(pl.multiple_of(g * 4 * HD, 4 * HD), 4 * HD))
        q = jnp.concatenate([q4[:, j * HD:(j + 1) * HD] for j in range(4)], axis=0)
        window = pl.ds(pl.multiple_of(b * BLK, BLK), WIN)
        k = kv[g, window, 0:HD]
        v = kv[g, window, HD:2 * HD]
        s = lax.dot_general(q, k, (((1,), (1,)), ((), ())), preferred_element_type=F32)
        st = st_ref[pl.ds(pl.multiple_of(b * BLK, BLK), BLK), :]
        far = lane[:, :14 * BLK] >= jnp.concatenate([st] * 14, axis=1)
        last = (lane[:, 14 * BLK:] >= st) & causal
        far4 = jnp.concatenate([far] * 4, axis=0)
        last4 = jnp.concatenate([last] * 4, axis=0)
        s = jnp.concatenate([jnp.where(far4, s[:, :14 * BLK], NEG),
                             jnp.where(last4, s[:, 14 * BLK:], NEG)], axis=1)
        m = jnp.max(s, axis=1, keepdims=True)
        p = jnp.exp2((s - m) * SCALE).astype(BF16)
        vo = jnp.concatenate([v, jnp.ones((WIN, HD), BF16)], axis=1)
        o = jnp.dot(p, vo, preferred_element_type=F32)
        a = (o[:, :HD] / o[:, HD:]).astype(BF16)
        a4 = jnp.concatenate([a[j * BLK:(j + 1) * BLK] for j in range(4)], axis=1)
        att[4 * h + g, pl.ds(pl.multiple_of(b * BLK, BLK), BLK), :] = a4
        return carry

    lax.fori_loop(0, 16, unit, 0)
    att_copy(h, 3, 3).start()

    @pl.when(x < EARLY)
    def _():
        both_parts(3)

    @pl.when(x >= EARLY)
    def _():
        def project_a(j, carry):
            d = lax.rem(lax.div(j + 1, 2) * (2 * lax.rem(j, 2) - 1) + 8, 8)
            at = lax.rem(z + 8 - d, 8)

            @pl.when(j == 7)
            def _():
                got(*az((0, 1, 2, 3), 3))
                go(am[7])

            for i in range(8):
                @pl.when(j == i)
                def _(i=i):
                    got(am[i])

            @pl.when(lax.div(at, 4) == 1 - h)
            def _():
                for b in range(4):
                    att_copy(1 - h, lax.rem(at, 4), b).wait_recv()

            acca[...] += jnp.dot(att[at], wa[at].reshape(ROWS, NA), preferred_element_type=F32)
            return carry

        lax.fori_loop(0, 8, project_a, 0)
        got(*bx(range(8), 2))
        go(bm[3])
        got(*bx(range(8), 0))
        go(bm[1])
        got(*bm)

        def project_b(at, carry):
            accb[...] += jnp.dot(att[at], wb[at].reshape(ROWS, NB), preferred_element_type=F32)
            return carry

        lax.fori_loop(0, 8, project_b, 0)

    def placed(ref, j):
        part = ref[3 * BLK:4 * BLK, :]
        for b in (2, 1, 0):
            part = jnp.where(order[j] == b, ref[b * BLK:(b + 1) * BLK, :], part)
        return part.astype(BF16)

    for j in range(4):
        out_ref[j * BLK:(j + 1) * BLK, 0:NA] = placed(acca, j)
        out_ref[j * BLK:(j + 1) * BLK, NA:2048] = placed(accb, j)

    for g in range(NG):
        kv_drain(g)
        for b in range(4):
            att_copy(h, g, b).wait_send()
    for copy, _, _ in ax + [ay, by] + am + bm:
        copy().wait_send()
    for s in range(4):
        for copy, _, _ in az((0, 1, 2, 3), s) + bz(s):
            copy().wait_send()
    for way in range(3):
        for copy, _, _ in bx(range(8), way):
            copy().wait_send()


def per_device(queries, key_states, value_rows_stored, span_order, doc_lengths, w_out):
    vmem = pl.BlockSpec(memory_space=pltpu.VMEM)
    return pl.pallas_call(
        kernel,
        out_shape=pltpu.VMEM((ROWS, 2048), BF16),
        in_specs=[pl.BlockSpec(memory_space=pltpu.SMEM), vmem, pl.BlockSpec(memory_space=pl.ANY), vmem, vmem, vmem],
        out_specs=vmem,
        scratch_shapes=[
            pltpu.VMEM((ROWS, 2048), BF16),
            pltpu.VMEM((NG, 18 * BLK, 2 * HD), BF16),
            pltpu.VMEM((max(1, len(VIA)), 4 * BLK, 2 * HD), BF16),
            pltpu.VMEM((NZ, NY, NX, 2, 32, NA), BF16),
            pltpu.VMEM((NZ, NY, NX, 2, 32, NB), BF16),
            pltpu.VMEM((8, ROWS, 4 * HD), BF16),
            pltpu.VMEM((ROWS, NA), F32),
            pltpu.VMEM((ROWS, NB), F32),
            pltpu.VMEM((ROWS, 128), F32),
            pltpu.SemaphoreType.DMA((NG, 5)),
            pltpu.SemaphoreType.DMA((NG, 4)),
            pltpu.SemaphoreType.DMA((max(1, len(VIA)),)),
            pltpu.SemaphoreType.DMA((max(1, len(VIA)),)),
            pltpu.SemaphoreType.DMA((N_W,)),
            pltpu.SemaphoreType.DMA((N_W,)),
            pltpu.SemaphoreType.DMA((NG, 4)),
            pltpu.SemaphoreType.DMA((NG, 4)),
            pltpu.SemaphoreType.DMA,
        ],
        compiler_params=pltpu.CompilerParams(
            collective_id=0, has_side_effects=True, vmem_limit_bytes=58 * 1024 * 1024),
        name="attend_project",
    )(span_order.T, doc_lengths.reshape(1, 128), queries, key_states, value_rows_stored, w_out)


def solution(mesh):
    placed = (P("ctx", "head"), P("ctx", "head"), P("ctx", "head"), P(), P(), P("ctx", "head"))
    return jax.shard_map(
        per_device, mesh=mesh, in_specs=placed, out_specs=P("ctx", "head"), check_vma=False
    )
```

```python
import math

import jax
import jax.numpy as jnp
from jax import lax
from jax.experimental import pallas as pl
from jax.experimental.pallas import tpu as pltpu
from jax.sharding import PartitionSpec as P

MESH = pl.DeviceIdType.MESH
BF16 = jnp.bfloat16
F32 = jnp.float32
HD = 128
BLK = 128
ROWS = 512
NX, NY, NZ = 4, 2, 8
NG = 4
WIN = 15 * BLK
NA = 1024
NB = 2048 - NA
SCALE = math.log2(math.e) / math.sqrt(HD)
NEG = -1e30

AX, AY, AZ, AM = 0, 3, 4, 32
BZ, BY, BX, BM = 40, 47, 48, 72
N_W = 76
VIA = (3,)
EARLY = 1


def kernel(so_ref, lens_ref, q_hbm, k_ref, v_ref, w_ref, out_ref,
           q_ref, kv, transit, wa, wb, att, acca, accb, st_ref, kvs, kvr, ts, tr, ws, wr, ats, atr, q_sem):
    q_copy = pltpu.make_async_copy(q_hbm, q_ref, q_sem)
    q_copy.start()
    c = lax.axis_index("ctx")
    h = lax.axis_index("head")
    core = lax.rem(c, 2)
    chip = lax.div(c, 2)
    x = lax.rem(chip, NX)
    yl = lax.rem(lax.div(chip, NX), NY)
    z = lax.div(chip, NX * NY)

    def dev(z_, y_, x_, core_, h_):
        return (((z_ * NY + y_) * NX + x_) * 2 + core_, h_)

    def along(by, core_):
        return (lax.rem(chip + by + 64, 64) * 2 + core_, h)

    def zz(by):
        return lax.rem(z + by + NZ, NZ)

    def xx(by):
        return lax.rem(x + by + NX, NX)

    mate = (chip * 2 + 1 - core, h)
    xp, xm = dev(z, yl, xx(1), core, h), dev(z, yl, xx(-1), core, h)
    zp, zm = dev(zz(1), yl, x, core, h), dev(zz(-1), yl, x, core, h)
    yo = dev(z, 1 - yl, x, core, h)
    ho = (c, 1 - h)

    barrier = pltpu.get_barrier_semaphore()

    def signal(to):
        pl.semaphore_signal(barrier, inc=1, device_id=to, device_id_type=MESH)

    for to in (mate, xp, xm, zp, zm, yo, ho, along(-1, core)):
        signal(to)

    @pl.when(core == 0)
    def _():
        signal(along(-1, 1))

    @pl.when(x == 0)
    def _():
        signal(along(-4, core))

    order = [so_ref[j, c] for j in range(4)]

    def held(ref, span, cols):
        parts = [ref[j * BLK:(j + 1) * BLK, cols] for j in range(4)]
        part = parts[3]
        for j in (2, 1, 0):
            part = jnp.where(order[j] == span, parts[j], part)
        return part

    for b in range(4):
        for g in range(NG):
            at = pl.ds((14 + b) * BLK, BLK)
            kv[g, at, 0:HD] = held(k_ref, b, slice(g * HD, (g + 1) * HD))
            kv[g, at, HD:2 * HD] = held(v_ref, b, slice(g * HD, (g + 1) * HD))
    wa[z, yl, x, core] = w_ref[:, 0:NA]
    wb[z, yl, x, core] = w_ref[:, NA:2048]

    lens = lens_ref[...]
    high = lax.div(lens, 64)
    low = lens - high * 64
    upto = (lax.broadcasted_iota(jnp.int32, (128, 128), 0)
            <= lax.broadcasted_iota(jnp.int32, (128, 128), 1)).astype(F32).astype(BF16)

    def running(part):
        wide = jnp.broadcast_to(part.astype(F32), (16, 128)).astype(BF16)
        return jnp.dot(wide, upto, preferred_element_type=F32)[0:1, :]

    ends = running(high) * 64.0 + running(low)
    pos = (lax.broadcasted_iota(jnp.int32, (ROWS, 128), 0) + c * ROWS).astype(F32)
    begun = jnp.where(ends <= pos, ends, 0.0)
    first = jnp.max(begun, axis=1, keepdims=True)
    blk = lax.div(lax.broadcasted_iota(jnp.int32, (ROWS, 128), 0), BLK)
    origin = (blk * BLK + (c * ROWS - 14 * BLK)).astype(F32)
    st_ref[...] = jnp.broadcast_to(first, (ROWS, 128)) - origin

    acca[...] = jnp.zeros_like(acca)
    accb[...] = jnp.zeros_like(accb)

    pl.semaphore_wait(barrier, 8 + core + jnp.where(x == 0, 1, 0))

    def kv_at(g, tile, tiles):
        return kv.at[g, pl.ds(tile * BLK, tiles * BLK)]

    def kv_copy(g, src, dst, tiles, number, slot, to):
        return pltpu.make_async_remote_copy(
            src_ref=kv_at(g, src, tiles), dst_ref=kv_at(g, dst, tiles),
            send_sem=kvs.at[g, number], recv_sem=kvr.at[g, slot],
            device_id=to, device_id_type=MESH)

    def own_near(g):
        return kv_copy(g, 14, 6, 4, 0, 1, along(1, core))

    def own_via(g):
        return pltpu.make_async_remote_copy(
            src_ref=kv_at(g, 14, 4), dst_ref=transit.at[VIA.index(g)],
            send_sem=kvs.at[g, 0], recv_sem=tr.at[VIA.index(g)], device_id=xp, device_id_type=MESH)

    def own_on(g):
        return pltpu.make_async_remote_copy(
            src_ref=transit.at[VIA.index(g)], dst_ref=kv_at(g, 6, 4),
            send_sem=ts.at[VIA.index(g)], recv_sem=kvr.at[g, 1], device_id=along(4, core),
            device_id_type=MESH)

    def own_mate(g):
        return kv_copy(g, 14, 10, 4, 1, 0, mate)

    def pass0(g):
        return [kv_copy(g, 8, 0, 2, 2, 3, along(1, 0)), kv_copy(g, 6, 2, 4, 3, 2, mate)]

    def pass1(g):
        return [kv_copy(g, 6, 2, 4, 2, 2, along(1, 0)), kv_copy(g, 6, 10, 4, 3, 0, mate)]

    def late0(g):
        return kv_copy(g, 4, 0, 2, 4, 3, mate)

    def kv_wait(g, slot):
        tile, tiles = ((10, 4), (6, 4), (2, 4), (0, 2))[slot]
        kv_copy(g, tile, tile, tiles, 0, slot, mate).wait_recv()

    def kv_send(g):
        if g in VIA:
            @pl.when(x < 3)
            def _():
                own_near(g).start()
        else:
            own_near(g).start()

        @pl.when(core == 0)
        def _():
            own_mate(g).start()

    def kv_via(g):
        if g not in VIA:
            return

        @pl.when(x == 3)
        def _():
            own_via(g).start()

    def kv_on(g):
        if g not in VIA:
            return

        @pl.when(x == 0)
        def _():
            own_via(g).wait_recv()
            own_on(g).start()

    def kv_pass(g):
        kv_wait(g, 1)

        @pl.when(core == 0)
        def _():
            for copy in pass0(g):
                copy.start()

        @pl.when(core == 1)
        def _():
            for copy in pass1(g):
                copy.start()

    def kv_late(g):
        kv_wait(g, 2)

        @pl.when(core == 0)
        def _():
            late0(g).start()

    def kv_rest(g):
        kv_wait(g, 0)
        kv_wait(g, 3)

    def kv_drain(g):
        own_near(g).wait_send()
        if g in VIA:
            @pl.when(x == 0)
            def _():
                own_on(g).wait_send()

        @pl.when(core == 0)
        def _():
            for copy in [own_mate(g)] + pass0(g) + [late0(g)]:
                copy.wait_send()

        @pl.when(core == 1)
        def _():
            for copy in pass1(g):
                copy.wait_send()

    def put(part, number, to, src=None):
        return lambda: pltpu.make_async_remote_copy(
            src_ref=part if src is None else src, dst_ref=part,
            send_sem=ws.at[number], recv_sem=wr.at[number], device_id=to, device_id_type=MESH)

    def entry(part, number, to, got_part, src=None):
        return put(part, number, to, src), number, got_part

    def a_block(y_):
        return wa.at[z, y_, x, core]

    def a_pair(x_):
        return wa.at[z, :, x_, core]

    def a_group(z_, core_=None):
        return wa.at[z_, :, :, core if core_ is None else core_]

    def b_block(y_):
        return wb.at[z, y_, x, core]

    def b_pair(z_):
        return wb.at[z_, :, x, core]

    def b_group(x_, core_=None):
        return wb.at[:, :, x_, core if core_ is None else core_]

    own_a, own_b = w_ref.at[:, pl.ds(0, NA)], w_ref.at[:, pl.ds(NA, NB)]
    ay = entry(a_block(yl), AY, yo, a_block(1 - yl), own_a)
    by = entry(b_block(yl), BY, yo, b_block(1 - yl), own_b)
    ax = [entry(a_pair(x), AX, xp, a_pair(xx(-1))),
          entry(a_pair(x), AX + 1, xm, a_pair(xx(1))),
          entry(a_pair(xx(1)), AX + 2, xm, a_pair(xx(2)))]
    xq = (x, xx(-1), xx(1), xx(2))

    def az(qs, s):
        def part(d, q):
            return wa.at[zz(d), :, xq[q], core]
        if s == 3:
            return [entry(part(3, q), AZ + 7 * q + 6, zm, part(4, q)) for q in qs]
        return ([entry(part(-s, q), AZ + 7 * q + 2 * s, zp, part(-s - 1, q)) for q in qs]
                + [entry(part(s, q), AZ + 7 * q + 2 * s + 1, zm, part(s + 1, q)) for q in qs])

    def bz(s):
        if s == 3:
            return [entry(b_pair(zz(3)), BZ + 6, zm, b_pair(zz(4)))]
        return [entry(b_pair(zz(-s)), BZ + 2 * s, zp, b_pair(zz(-s - 1))),
                entry(b_pair(zz(s)), BZ + 2 * s + 1, zm, b_pair(zz(s + 1)))]

    near = (0, -1, 1, -2, 2, -3, 3, 4)
    am = [entry(a_group(zz(d)), AM + i, mate, a_group(zz(d), 1 - core)) for i, d in enumerate(near)]

    def bx(js, way):
        def part(j, d):
            return wb.at[zz(near[j]), :, xx(d), core]
        if way == 0:
            return [entry(part(j, 0), BX + 3 * j, xp, part(j, -1)) for j in js]
        if way == 1:
            return [entry(part(j, 0), BX + 3 * j + 1, xm, part(j, 1)) for j in js]
        return [entry(part(j, 1), BX + 3 * j + 2, xm, part(j, 2)) for j in js]

    bm = [entry(b_group(xx(d)), BM + i, mate, b_group(xx(d), 1 - core))
          for i, d in enumerate((0, -1, 1, 2))]

    def go(*entries):
        for copy, _, _ in entries:
            copy().start()

    def got(*entries):
        for _, number, part in entries:
            put(part, number, mate)().wait_recv()

    def att_copy(head, g, b):
        part = att.at[4 * head + g, pl.ds(b * BLK, BLK)]
        return pltpu.make_async_remote_copy(
            src_ref=part, dst_ref=part, send_sem=ats.at[g, b], recv_sem=atr.at[g, b],
            device_id=ho, device_id_type=MESH)

    go(ay, by)
    kv_send(0)
    kv_send(1)
    got(ay, by)
    go(ax[1], *bz(0), *az((0,), 0), *bx((0,), 1))
    kv_pass(0)
    go(ax[0])
    kv_send(2)
    kv_via(2)
    kv_via(3)
    got(ax[1])
    go(ax[2], *az((2,), 0))
    got(*bz(0))
    go(*bz(1), *bx((1, 2), 1))
    kv_pass(1)
    kv_send(3)
    got(*bz(1))
    go(*bz(2), *bx((3, 4), 1))
    got(ax[2])
    go(*az((3,), 0))
    q_copy.wait()
    kv_late(0)

    def at1():
        got(*bz(2))
        go(*bz(3), *bx((5, 6), 1))
        got(*az((0,), 0))
        go(*az((0,), 1))
        got(ax[0])
        go(*az((1,), 0), am[0])

    def at2():
        kv_on(2)
        kv_on(3)
        got(*bz(3))
        go(*bx((7,), 1), bm[0])

    def at3():
        got(*az((2, 3), 0))
        go(*az((2, 3), 1))
        kv_late(1)

        @pl.when(x > 0)
        def _():
            kv_pass(2)

    def at4():
        got(*az((1,), 0))
        go(*az((1,), 1), am[1], am[2])
        got(*bx((0, 1, 2, 3), 1))
        go(*bx((0, 1, 2, 3), 2))
        @pl.when(x == 0)
        def _():
            kv_pass(2)

        go(*bx((0, 1), 0))

    def at6():
        got(*az((0, 2), 1))
        go(*az((0, 2), 2))

        @pl.when(x > 0)
        def _():
            kv_pass(3)

    def at7():
        got(*az((3, 1), 1))
        go(*az((3, 1), 2), am[3], am[4])
        got(*bx((4, 5, 6, 7), 1))
        go(*bx((4, 5, 6, 7), 2), bm[2])
        kv_late(2)

    def at8():
        @pl.when(x == 0)
        def _():
            kv_pass(3)

        go(*bx((2, 3, 4, 5, 6, 7), 0))

    def at9():
        got(*az((0, 2), 2))
        go(*az((0, 2), 3))

    def at11():
        got(*az((3, 1), 2))
        go(*az((3, 1), 3), am[5], am[6])
        kv_late(3)

    before = {1: at1, 2: at2, 3: at3, 4: at4, 6: at6, 7: at7, 8: at8, 9: at9, 11: at11}

    def both_parts(g):
        def part(at):
            a = att[at]
            acca[...] += jnp.dot(a, wa[at].reshape(ROWS, NA), preferred_element_type=F32)
            accb[...] += jnp.dot(a, wb[at].reshape(ROWS, NB), preferred_element_type=F32)

        def side(k, carry):
            head = lax.rem(h + k, 2)

            @pl.when(k == 1)
            def _():
                for b in range(4):
                    att_copy(1 - h, g, b).wait_recv()

            part(4 * head + g)
            return carry

        lax.fori_loop(0, 2, side, 0)

    def project_early():
        got(*az((0, 1, 2, 3), 3))
        go(am[7])
        got(*bx(range(8), 2))
        go(bm[3])
        got(*bx(range(8), 0))
        go(bm[1])
        got(*am)
        got(*bm)

        def each(g, carry):
            both_parts(g)
            return carry

        lax.fori_loop(0, 3, each, 0)

    lane = lax.broadcasted_iota(jnp.int32, (BLK, WIN), 1).astype(F32)
    row = lax.broadcasted_iota(jnp.int32, (BLK, BLK), 0)
    causal = lax.broadcasted_iota(jnp.int32, (BLK, BLK), 1) <= row

    def unit(i, carry):
        g, b = lax.div(i, 4), lax.rem(i, 4)
        @pl.when(i > 0)
        def _():
            att_copy(h, lax.div(i - 1, 4), lax.rem(i - 1, 4)).start()

        for at, run in before.items():
            pl.when(i == at)(run)

        @pl.when((i == 12) & (x < EARLY))
        def _():
            project_early()


        @pl.when(b == 0)
        def _():
            kv_rest(g)

        q4 = held(q_ref, b, pl.ds(pl.multiple_of(g * 4 * HD, 4 * HD), 4 * HD))
        q = jnp.concatenate([q4[:, j * HD:(j + 1) * HD] for j in range(4)], axis=0)
        window = pl.ds(pl.multiple_of(b * BLK, BLK), WIN)
        k = kv[g, window, 0:HD]
        v = kv[g, window, HD:2 * HD]
        s = lax.dot_general(q, k, (((1,), (1,)), ((), ())), preferred_element_type=F32)
        st = st_ref[pl.ds(pl.multiple_of(b * BLK, BLK), BLK), :]
        far = lane[:, :14 * BLK] >= jnp.concatenate([st] * 14, axis=1)
        last = (lane[:, 14 * BLK:] >= st) & causal
        far4 = jnp.concatenate([far] * 4, axis=0)
        last4 = jnp.concatenate([last] * 4, axis=0)
        s = jnp.concatenate([jnp.where(far4, s[:, :14 * BLK], NEG),
                             jnp.where(last4, s[:, 14 * BLK:], NEG)], axis=1)
        m = jnp.max(s, axis=1, keepdims=True)
        p = jnp.exp2((s - m) * SCALE).astype(BF16)
        vo = jnp.concatenate([v, jnp.ones((WIN, HD), BF16)], axis=1)
        o = jnp.dot(p, vo, preferred_element_type=F32)
        a = (o[:, :HD] / o[:, HD:]).astype(BF16)
        a4 = jnp.concatenate([a[j * BLK:(j + 1) * BLK] for j in range(4)], axis=1)
        att[4 * h + g, pl.ds(pl.multiple_of(b * BLK, BLK), BLK), :] = a4
        return carry

    lax.fori_loop(0, 16, unit, 0)
    att_copy(h, 3, 3).start()

    @pl.when(x < EARLY)
    def _():
        both_parts(3)

    @pl.when(x >= EARLY)
    def _():
        def project_a(j, carry):
            d = lax.rem(lax.div(j + 1, 2) * (2 * lax.rem(j, 2) - 1) + 8, 8)
            at = lax.rem(z + 8 - d, 8)

            @pl.when(j == 7)
            def _():
                got(*az((0, 1, 2, 3), 3))
                go(am[7])

            for i in range(8):
                @pl.when(j == i)
                def _(i=i):
                    got(am[i])

            @pl.when(lax.div(at, 4) == 1 - h)
            def _():
                for b in range(4):
                    att_copy(1 - h, lax.rem(at, 4), b).wait_recv()

            acca[...] += jnp.dot(att[at], wa[at].reshape(ROWS, NA), preferred_element_type=F32)
            return carry

        lax.fori_loop(0, 8, project_a, 0)
        got(*bx(range(8), 2))
        go(bm[3])
        got(*bx(range(8), 0))
        go(bm[1])
        got(*bm)

        def project_b(at, carry):
            accb[...] += jnp.dot(att[at], wb[at].reshape(ROWS, NB), preferred_element_type=F32)
            return carry

        lax.fori_loop(0, 8, project_b, 0)

    def placed(ref, j):
        part = ref[3 * BLK:4 * BLK, :]
        for b in (2, 1, 0):
            part = jnp.where(order[j] == b, ref[b * BLK:(b + 1) * BLK, :], part)
        return part.astype(BF16)

    for j in range(4):
        out_ref[j * BLK:(j + 1) * BLK, 0:NA] = placed(acca, j)
        out_ref[j * BLK:(j + 1) * BLK, NA:2048] = placed(accb, j)

    for g in range(NG):
        kv_drain(g)
        for b in range(4):
            att_copy(h, g, b).wait_send()
    for copy, _, _ in ax + [ay, by] + am + bm:
        copy().wait_send()
    for s in range(4):
        for copy, _, _ in az((0, 1, 2, 3), s) + bz(s):
            copy().wait_send()
    for way in range(3):
        for copy, _, _ in bx(range(8), way):
            copy().wait_send()


def per_device(queries, key_states, value_rows_stored, span_order, doc_lengths, w_out):
    vmem = pl.BlockSpec(memory_space=pltpu.VMEM)
    return pl.pallas_call(
        kernel,
        out_shape=pltpu.VMEM((ROWS, 2048), BF16),
        in_specs=[pl.BlockSpec(memory_space=pltpu.SMEM), vmem, pl.BlockSpec(memory_space=pl.ANY), vmem, vmem, vmem],
        out_specs=vmem,
        scratch_shapes=[
            pltpu.VMEM((ROWS, 2048), BF16),
            pltpu.VMEM((NG, 18 * BLK, 2 * HD), BF16),
            pltpu.VMEM((max(1, len(VIA)), 4 * BLK, 2 * HD), BF16),
            pltpu.VMEM((NZ, NY, NX, 2, 32, NA), BF16),
            pltpu.VMEM((NZ, NY, NX, 2, 32, NB), BF16),
            pltpu.VMEM((8, ROWS, 4 * HD), BF16),
            pltpu.VMEM((ROWS, NA), F32),
            pltpu.VMEM((ROWS, NB), F32),
            pltpu.VMEM((ROWS, 128), F32),
            pltpu.SemaphoreType.DMA((NG, 5)),
            pltpu.SemaphoreType.DMA((NG, 4)),
            pltpu.SemaphoreType.DMA((max(1, len(VIA)),)),
            pltpu.SemaphoreType.DMA((max(1, len(VIA)),)),
            pltpu.SemaphoreType.DMA((N_W,)),
            pltpu.SemaphoreType.DMA((N_W,)),
            pltpu.SemaphoreType.DMA((NG, 4)),
            pltpu.SemaphoreType.DMA((NG, 4)),
            pltpu.SemaphoreType.DMA,
        ],
        compiler_params=pltpu.CompilerParams(
            collective_id=0, has_side_effects=True, vmem_limit_bytes=58 * 1024 * 1024),
        name="attend_project",
    )(span_order.T, doc_lengths.reshape(1, 128), queries, key_states, value_rows_stored, w_out)


def solution(mesh):
    placed = (P("ctx", "head"), P("ctx", "head"), P("ctx", "head"), P(), P(), P("ctx", "head"))
    return jax.shard_map(
        per_device, mesh=mesh, in_specs=placed, out_specs=P("ctx", "head"), check_vma=False
    )
```

```python
import math

import jax
import jax.numpy as jnp
from jax import lax
from jax.experimental import pallas as pl
from jax.experimental.pallas import tpu as pltpu
from jax.sharding import PartitionSpec as P

MESH = pl.DeviceIdType.MESH
BF16 = jnp.bfloat16
F32 = jnp.float32
HD = 128
BLK = 128
ROWS = 512
NX, NY, NZ = 4, 2, 8
NG = 4
WIN = 15 * BLK
NA = 1024
NB = 2048 - NA
SCALE = math.log2(math.e) / math.sqrt(HD)
NEG = -1e30

AX, AY, AZ, AM = 0, 3, 4, 32
BZ, BY, BX, BM = 40, 47, 48, 72
N_W = 76
VIA = (3,)
EARLY = 1


def kernel(so_ref, lens_ref, q_hbm, k_ref, v_ref, w_ref, out_ref,
           q_ref, kv, transit, wa, wb, att, acca, accb, st_ref, kvs, kvr, ts, tr, ws, wr, ats, atr, q_sem):
    q_copy = pltpu.make_async_copy(q_hbm, q_ref, q_sem)
    q_copy.start()
    c = lax.axis_index("ctx")
    h = lax.axis_index("head")
    core = lax.rem(c, 2)
    chip = lax.div(c, 2)
    x = lax.rem(chip, NX)
    yl = lax.rem(lax.div(chip, NX), NY)
    z = lax.div(chip, NX * NY)

    def dev(z_, y_, x_, core_, h_):
        return (((z_ * NY + y_) * NX + x_) * 2 + core_, h_)

    def along(by, core_):
        return (lax.rem(chip + by + 64, 64) * 2 + core_, h)

    def zz(by):
        return lax.rem(z + by + NZ, NZ)

    def xx(by):
        return lax.rem(x + by + NX, NX)

    mate = (chip * 2 + 1 - core, h)
    xp, xm = dev(z, yl, xx(1), core, h), dev(z, yl, xx(-1), core, h)
    zp, zm = dev(zz(1), yl, x, core, h), dev(zz(-1), yl, x, core, h)
    yo = dev(z, 1 - yl, x, core, h)
    ho = (c, 1 - h)

    barrier = pltpu.get_barrier_semaphore()

    def signal(to):
        pl.semaphore_signal(barrier, inc=1, device_id=to, device_id_type=MESH)

    for to in (mate, xp, xm, zp, zm, yo, ho, along(-1, core)):
        signal(to)

    @pl.when(core == 0)
    def _():
        signal(along(-1, 1))

    @pl.when(x == 0)
    def _():
        signal(along(-4, core))

    order = [so_ref[j, c] for j in range(4)]

    def held(ref, span, cols):
        parts = [ref[j * BLK:(j + 1) * BLK, cols] for j in range(4)]
        part = parts[3]
        for j in (2, 1, 0):
            part = jnp.where(order[j] == span, parts[j], part)
        return part

    for b in range(4):
        for g in range(NG):
            at = pl.ds((14 + b) * BLK, BLK)
            kv[g, at, 0:HD] = held(k_ref, b, slice(g * HD, (g + 1) * HD))
            kv[g, at, HD:2 * HD] = held(v_ref, b, slice(g * HD, (g + 1) * HD))
    wa[z, yl, x, core] = w_ref[:, 0:NA]
    wb[z, yl, x, core] = w_ref[:, NA:2048]

    lens = lens_ref[...]
    high = lax.div(lens, 64)
    low = lens - high * 64
    upto = (lax.broadcasted_iota(jnp.int32, (128, 128), 0)
            <= lax.broadcasted_iota(jnp.int32, (128, 128), 1)).astype(F32).astype(BF16)

    def running(part):
        wide = jnp.broadcast_to(part.astype(F32), (16, 128)).astype(BF16)
        return jnp.dot(wide, upto, preferred_element_type=F32)[0:1, :]

    ends = running(high) * 64.0 + running(low)
    pos = (lax.broadcasted_iota(jnp.int32, (ROWS, 128), 0) + c * ROWS).astype(F32)
    begun = jnp.where(ends <= pos, ends, 0.0)
    first = jnp.max(begun, axis=1, keepdims=True)
    blk = lax.div(lax.broadcasted_iota(jnp.int32, (ROWS, 128), 0), BLK)
    origin = (blk * BLK + (c * ROWS - 14 * BLK)).astype(F32)
    st_ref[...] = jnp.broadcast_to(first, (ROWS, 128)) - origin

    acca[...] = jnp.zeros_like(acca)
    accb[...] = jnp.zeros_like(accb)

    pl.semaphore_wait(barrier, 8 + core + jnp.where(x == 0, 1, 0))

    def kv_at(g, tile, tiles):
        return kv.at[g, pl.ds(tile * BLK, tiles * BLK)]

    def kv_copy(g, src, dst, tiles, number, slot, to):
        return pltpu.make_async_remote_copy(
            src_ref=kv_at(g, src, tiles), dst_ref=kv_at(g, dst, tiles),
            send_sem=kvs.at[g, number], recv_sem=kvr.at[g, slot],
            device_id=to, device_id_type=MESH)

    def own_near(g):
        return kv_copy(g, 14, 6, 4, 0, 1, along(1, core))

    def own_via(g):
        return pltpu.make_async_remote_copy(
            src_ref=kv_at(g, 14, 4), dst_ref=transit.at[VIA.index(g)],
            send_sem=kvs.at[g, 0], recv_sem=tr.at[VIA.index(g)], device_id=xp, device_id_type=MESH)

    def own_on(g):
        return pltpu.make_async_remote_copy(
            src_ref=transit.at[VIA.index(g)], dst_ref=kv_at(g, 6, 4),
            send_sem=ts.at[VIA.index(g)], recv_sem=kvr.at[g, 1], device_id=along(4, core),
            device_id_type=MESH)

    def own_mate(g):
        return kv_copy(g, 14, 10, 4, 1, 0, mate)

    def pass0(g):
        return [kv_copy(g, 8, 0, 2, 2, 3, along(1, 0)), kv_copy(g, 6, 2, 4, 3, 2, mate)]

    def pass1(g):
        return [kv_copy(g, 6, 2, 4, 2, 2, along(1, 0)), kv_copy(g, 6, 10, 4, 3, 0, mate)]

    def late0(g):
        return kv_copy(g, 4, 0, 2, 4, 3, mate)

    def kv_wait(g, slot):
        tile, tiles = ((10, 4), (6, 4), (2, 4), (0, 2))[slot]
        kv_copy(g, tile, tile, tiles, 0, slot, mate).wait_recv()

    def kv_send(g):
        if g in VIA:
            @pl.when(x < 3)
            def _():
                own_near(g).start()
        else:
            own_near(g).start()

        @pl.when(core == 0)
        def _():
            own_mate(g).start()

    def kv_via(g):
        if g not in VIA:
            return

        @pl.when(x == 3)
        def _():
            own_via(g).start()

    def kv_on(g):
        if g not in VIA:
            return

        @pl.when(x == 0)
        def _():
            own_via(g).wait_recv()
            own_on(g).start()

    def kv_pass(g):
        kv_wait(g, 1)

        @pl.when(core == 0)
        def _():
            for copy in pass0(g):
                copy.start()

        @pl.when(core == 1)
        def _():
            for copy in pass1(g):
                copy.start()

    def kv_late(g):
        kv_wait(g, 2)

        @pl.when(core == 0)
        def _():
            late0(g).start()

    def kv_rest(g):
        kv_wait(g, 0)
        kv_wait(g, 3)

    def kv_drain(g):
        own_near(g).wait_send()
        if g in VIA:
            @pl.when(x == 0)
            def _():
                own_on(g).wait_send()

        @pl.when(core == 0)
        def _():
            for copy in [own_mate(g)] + pass0(g) + [late0(g)]:
                copy.wait_send()

        @pl.when(core == 1)
        def _():
            for copy in pass1(g):
                copy.wait_send()

    def put(part, number, to, src=None):
        return lambda: pltpu.make_async_remote_copy(
            src_ref=part if src is None else src, dst_ref=part,
            send_sem=ws.at[number], recv_sem=wr.at[number], device_id=to, device_id_type=MESH)

    def entry(part, number, to, got_part, src=None):
        return put(part, number, to, src), number, got_part

    def a_block(y_):
        return wa.at[z, y_, x, core]

    def a_pair(x_):
        return wa.at[z, :, x_, core]

    def a_group(z_, core_=None):
        return wa.at[z_, :, :, core if core_ is None else core_]

    def b_block(y_):
        return wb.at[z, y_, x, core]

    def b_pair(z_):
        return wb.at[z_, :, x, core]

    def b_group(x_, core_=None):
        return wb.at[:, :, x_, core if core_ is None else core_]

    own_a, own_b = w_ref.at[:, pl.ds(0, NA)], w_ref.at[:, pl.ds(NA, NB)]
    ay = entry(a_block(yl), AY, yo, a_block(1 - yl), own_a)
    by = entry(b_block(yl), BY, yo, b_block(1 - yl), own_b)
    ax = [entry(a_pair(x), AX, xp, a_pair(xx(-1))),
          entry(a_pair(x), AX + 1, xm, a_pair(xx(1))),
          entry(a_pair(xx(1)), AX + 2, xm, a_pair(xx(2)))]
    xq = (x, xx(-1), xx(1), xx(2))

    def az(qs, s):
        def part(d, q):
            return wa.at[zz(d), :, xq[q], core]
        if s == 3:
            return [entry(part(3, q), AZ + 7 * q + 6, zm, part(4, q)) for q in qs]
        return ([entry(part(-s, q), AZ + 7 * q + 2 * s, zp, part(-s - 1, q)) for q in qs]
                + [entry(part(s, q), AZ + 7 * q + 2 * s + 1, zm, part(s + 1, q)) for q in qs])

    def bz(s):
        if s == 3:
            return [entry(b_pair(zz(3)), BZ + 6, zm, b_pair(zz(4)))]
        return [entry(b_pair(zz(-s)), BZ + 2 * s, zp, b_pair(zz(-s - 1))),
                entry(b_pair(zz(s)), BZ + 2 * s + 1, zm, b_pair(zz(s + 1)))]

    near = (0, -1, 1, -2, 2, -3, 3, 4)
    am = [entry(a_group(zz(d)), AM + i, mate, a_group(zz(d), 1 - core)) for i, d in enumerate(near)]

    def bx(js, way):
        def part(j, d):
            return wb.at[zz(near[j]), :, xx(d), core]
        if way == 0:
            return [entry(part(j, 0), BX + 3 * j, xp, part(j, -1)) for j in js]
        if way == 1:
            return [entry(part(j, 0), BX + 3 * j + 1, xm, part(j, 1)) for j in js]
        return [entry(part(j, 1), BX + 3 * j + 2, xm, part(j, 2)) for j in js]

    bm = [entry(b_group(xx(d)), BM + i, mate, b_group(xx(d), 1 - core))
          for i, d in enumerate((0, -1, 1, 2))]

    def go(*entries):
        for copy, _, _ in entries:
            copy().start()

    def got(*entries):
        for _, number, part in entries:
            put(part, number, mate)().wait_recv()

    def att_copy(head, g, b):
        part = att.at[4 * head + g, pl.ds(b * BLK, BLK)]
        return pltpu.make_async_remote_copy(
            src_ref=part, dst_ref=part, send_sem=ats.at[g, b], recv_sem=atr.at[g, b],
            device_id=ho, device_id_type=MESH)

    go(ay, by)
    kv_send(0)
    kv_send(1)
    got(ay, by)
    go(ax[1], *bz(0), *az((0,), 0), *bx((0,), 1))
    kv_pass(0)
    go(ax[0])
    kv_send(2)
    kv_via(2)
    kv_via(3)
    got(ax[1])
    go(ax[2], *az((2,), 0))
    got(*bz(0))
    go(*bz(1), *bx((1, 2), 1))
    kv_pass(1)
    kv_send(3)
    got(*bz(1))
    go(*bz(2), *bx((3, 4), 1))
    got(ax[2])
    go(*az((3,), 0))
    q_copy.wait()
    kv_late(0)

    def at1():
        got(*bz(2))
        go(*bz(3), *bx((5, 6), 1))
        got(*az((0,), 0))
        go(*az((0,), 1))
        got(ax[0])
        go(*az((1,), 0), am[0])

    def at2():
        kv_on(2)
        kv_on(3)
        got(*bz(3))
        go(*bx((7,), 1), bm[0])

    def at3():
        got(*az((2, 3), 0))
        go(*az((2, 3), 1))
        kv_late(1)

        kv_pass(2)

    def at4():
        got(*az((1,), 0))
        go(*az((1,), 1), am[1], am[2])
        got(*bx((0, 1, 2, 3), 1))
        go(*bx((0, 1, 2, 3), 2))
        go(*bx((0, 1), 0))

    def at6():
        got(*az((0, 2), 1))
        go(*az((0, 2), 2))

        @pl.when(x > 0)
        def _():
            kv_pass(3)

    def at7():
        got(*az((3, 1), 1))
        go(*az((3, 1), 2), am[3], am[4])
        got(*bx((4, 5, 6, 7), 1))
        go(*bx((4, 5, 6, 7), 2), bm[2])
        kv_late(2)

        @pl.when(x == 0)
        def _():
            kv_pass(3)

    def at8():
        go(*bx((2, 3, 4, 5, 6, 7), 0))

    def at9():
        got(*az((0, 2), 2))
        go(*az((0, 2), 3))

    def at11():
        got(*az((3, 1), 2))
        go(*az((3, 1), 3), am[5], am[6])
        kv_late(3)

    before = {1: at1, 2: at2, 3: at3, 4: at4, 6: at6, 7: at7, 8: at8, 9: at9, 11: at11}

    def both_parts(g):
        def part(at):
            a = att[at]
            acca[...] += jnp.dot(a, wa[at].reshape(ROWS, NA), preferred_element_type=F32)
            accb[...] += jnp.dot(a, wb[at].reshape(ROWS, NB), preferred_element_type=F32)

        def side(k, carry):
            head = lax.rem(h + k, 2)

            @pl.when(k == 1)
            def _():
                for b in range(4):
                    att_copy(1 - h, g, b).wait_recv()

            part(4 * head + g)
            return carry

        lax.fori_loop(0, 2, side, 0)

    def project_early():
        got(*az((0, 1, 2, 3), 3))
        go(am[7])
        got(*bx(range(8), 2))
        go(bm[3])
        got(*bx(range(8), 0))
        go(bm[1])
        got(*am)
        got(*bm)

        def each(g, carry):
            both_parts(g)
            return carry

        lax.fori_loop(0, 3, each, 0)

    lane = lax.broadcasted_iota(jnp.int32, (BLK, WIN), 1).astype(F32)
    row = lax.broadcasted_iota(jnp.int32, (BLK, BLK), 0)
    causal = lax.broadcasted_iota(jnp.int32, (BLK, BLK), 1) <= row

    def unit(i, carry):
        g, b = lax.div(i, 4), lax.rem(i, 4)
        @pl.when(i > 0)
        def _():
            att_copy(h, lax.div(i - 1, 4), lax.rem(i - 1, 4)).start()

        for at, run in before.items():
            pl.when(i == at)(run)

        @pl.when((i == 12) & (x < EARLY))
        def _():
            project_early()


        @pl.when(b == 0)
        def _():
            kv_rest(g)

        q4 = held(q_ref, b, pl.ds(pl.multiple_of(g * 4 * HD, 4 * HD), 4 * HD))
        q = jnp.concatenate([q4[:, j * HD:(j + 1) * HD] for j in range(4)], axis=0)
        window = pl.ds(pl.multiple_of(b * BLK, BLK), WIN)
        k = kv[g, window, 0:HD]
        v = kv[g, window, HD:2 * HD]
        s = lax.dot_general(q, k, (((1,), (1,)), ((), ())), preferred_element_type=F32)
        st = st_ref[pl.ds(pl.multiple_of(b * BLK, BLK), BLK), :]
        far = lane[:, :14 * BLK] >= jnp.concatenate([st] * 14, axis=1)
        last = (lane[:, 14 * BLK:] >= st) & causal
        far4 = jnp.concatenate([far] * 4, axis=0)
        last4 = jnp.concatenate([last] * 4, axis=0)
        s = jnp.concatenate([jnp.where(far4, s[:, :14 * BLK], NEG),
                             jnp.where(last4, s[:, 14 * BLK:], NEG)], axis=1)
        m = jnp.max(s, axis=1, keepdims=True)
        p = jnp.exp2((s - m) * SCALE).astype(BF16)
        vo = jnp.concatenate([v, jnp.ones((WIN, HD), BF16)], axis=1)
        o = jnp.dot(p, vo, preferred_element_type=F32)
        a = (o[:, :HD] / o[:, HD:]).astype(BF16)
        a4 = jnp.concatenate([a[j * BLK:(j + 1) * BLK] for j in range(4)], axis=1)
        att[4 * h + g, pl.ds(pl.multiple_of(b * BLK, BLK), BLK), :] = a4
        return carry

    lax.fori_loop(0, 16, unit, 0)
    att_copy(h, 3, 3).start()

    @pl.when(x < EARLY)
    def _():
        both_parts(3)

    @pl.when(x >= EARLY)
    def _():
        def project_a(j, carry):
            d = lax.rem(lax.div(j + 1, 2) * (2 * lax.rem(j, 2) - 1) + 8, 8)
            at = lax.rem(z + 8 - d, 8)

            @pl.when(j == 7)
            def _():
                got(*az((0, 1, 2, 3), 3))
                go(am[7])

            for i in range(8):
                @pl.when(j == i)
                def _(i=i):
                    got(am[i])

            @pl.when(lax.div(at, 4) == 1 - h)
            def _():
                for b in range(4):
                    att_copy(1 - h, lax.rem(at, 4), b).wait_recv()

            acca[...] += jnp.dot(att[at], wa[at].reshape(ROWS, NA), preferred_element_type=F32)
            return carry

        lax.fori_loop(0, 8, project_a, 0)
        got(*bx(range(8), 2))
        go(bm[3])
        got(*bx(range(8), 0))
        go(bm[1])
        got(*bm)

        def project_b(at, carry):
            accb[...] += jnp.dot(att[at], wb[at].reshape(ROWS, NB), preferred_element_type=F32)
            return carry

        lax.fori_loop(0, 8, project_b, 0)

    def placed(ref, j):
        part = ref[3 * BLK:4 * BLK, :]
        for b in (2, 1, 0):
            part = jnp.where(order[j] == b, ref[b * BLK:(b + 1) * BLK, :], part)
        return part.astype(BF16)

    for j in range(4):
        out_ref[j * BLK:(j + 1) * BLK, 0:NA] = placed(acca, j)
        out_ref[j * BLK:(j + 1) * BLK, NA:2048] = placed(accb, j)

    for g in range(NG):
        kv_drain(g)
        for b in range(4):
            att_copy(h, g, b).wait_send()
    for copy, _, _ in ax + [ay, by] + am + bm:
        copy().wait_send()
    for s in range(4):
        for copy, _, _ in az((0, 1, 2, 3), s) + bz(s):
            copy().wait_send()
    for way in range(3):
        for copy, _, _ in bx(range(8), way):
            copy().wait_send()


def per_device(queries, key_states, value_rows_stored, span_order, doc_lengths, w_out):
    vmem = pl.BlockSpec(memory_space=pltpu.VMEM)
    return pl.pallas_call(
        kernel,
        out_shape=pltpu.VMEM((ROWS, 2048), BF16),
        in_specs=[pl.BlockSpec(memory_space=pltpu.SMEM), vmem, pl.BlockSpec(memory_space=pl.ANY), vmem, vmem, vmem],
        out_specs=vmem,
        scratch_shapes=[
            pltpu.VMEM((ROWS, 2048), BF16),
            pltpu.VMEM((NG, 18 * BLK, 2 * HD), BF16),
            pltpu.VMEM((max(1, len(VIA)), 4 * BLK, 2 * HD), BF16),
            pltpu.VMEM((NZ, NY, NX, 2, 32, NA), BF16),
            pltpu.VMEM((NZ, NY, NX, 2, 32, NB), BF16),
            pltpu.VMEM((8, ROWS, 4 * HD), BF16),
            pltpu.VMEM((ROWS, NA), F32),
            pltpu.VMEM((ROWS, NB), F32),
            pltpu.VMEM((ROWS, 128), F32),
            pltpu.SemaphoreType.DMA((NG, 5)),
            pltpu.SemaphoreType.DMA((NG, 4)),
            pltpu.SemaphoreType.DMA((max(1, len(VIA)),)),
            pltpu.SemaphoreType.DMA((max(1, len(VIA)),)),
            pltpu.SemaphoreType.DMA((N_W,)),
            pltpu.SemaphoreType.DMA((N_W,)),
            pltpu.SemaphoreType.DMA((NG, 4)),
            pltpu.SemaphoreType.DMA((NG, 4)),
            pltpu.SemaphoreType.DMA,
        ],
        compiler_params=pltpu.CompilerParams(
            collective_id=0, has_side_effects=True, vmem_limit_bytes=58 * 1024 * 1024),
        name="attend_project",
    )(span_order.T, doc_lengths.reshape(1, 128), queries, key_states, value_rows_stored, w_out)


def solution(mesh):
    placed = (P("ctx", "head"), P("ctx", "head"), P("ctx", "head"), P(), P(), P("ctx", "head"))
    return jax.shard_map(
        per_device, mesh=mesh, in_specs=placed, out_specs=P("ctx", "head"), check_vma=False
    )
```
